32 devices in a mesh: grp: 2 (over y), node: 4 (over z), sub: 2 (over x), rep: 2 (over core).
Axes of the slice: x: 2, y: 2, z: 4, core: 2. Of those that a mesh axis runs over, the one named last changes fastest.
Arguments:
- meson_nodes: float32 [2, 16, 512, 512], P(None, ('grp', 'node'), 'sub', 'rep'), parts along dimension 1, may hold values from -0.66 to 0.66
- term_nodes: int32 [8, 2], P('grp'), parts along dimension 0, may hold values from 0 to 7, as said below
- weight_codes: int32 [8], P('grp'), parts along dimension 0, may hold values from 0 to 7
- resident_pick: int32 [16], P('grp'), parts along dimension 0, may hold values from 0 to 1
Outputs:
- contracted: float32 [2, 16, 512, 512], P(None, ('grp', 'node'), 'sub', 'rep'), parts along dimension 1
The draws below stay inside these ranges and needn't reach their ends.
There are 2 independent parts, one for each index of `grp`. The reference program is written for one: setup_inputs(seed, part) draws one part's arguments, and reference() takes and returns one part's arrays. A program takes and returns all parts, laid end to end along the dimension named above; each array names one. Nothing has to cross between parts.
Inputs may be any that keep to these rules, and one draw needn't show every extreme that they name: `term_nodes`: node n belongs to owner n // 2. In every term the two nodes differ. The first nodes of at most 2 terms belong to any one owner, and those of exactly 2 terms to some owner.
All inputs are finite; a program needn't handle non-finite values.
Results may differ from the reference program's by a relative error of at most 0.000098.
Values sent between devices are 32-bit elements; how exact they have to be, the bound alone decides.
A program may use at most 64 MiB of HBM per device.

```python
import jax
import jax.numpy as jnp
from jax import lax

NODE_DEV = 2
ORDER = 512
SLOTS = 2
NODES = 8
TERMS = 4


def draw_term_nodes(key, part):
    owners = NODES // NODE_DEV
    key_bias, key_jitter, key_hot, key_order, key_local, key_other = jax.random.split(key, 6)
    levels = jax.random.randint(key_bias, (owners, 1), 0, 4) * 1024
    jitter = jax.random.randint(key_jitter, (owners, SLOTS), 0, 1024)
    hottest = jax.random.randint(key_hot, (), 0, owners)
    owner_grid = jnp.arange(owners, dtype=jnp.int32)[:, None] * jnp.ones((1, SLOTS), jnp.int32)
    scores = jnp.where(owner_grid == hottest, 4096, levels + jitter)
    unique = scores * (owners * SLOTS) + jnp.arange(owners * SLOTS, dtype=jnp.int32).reshape(owners, SLOTS)
    chosen = lax.top_k(unique.reshape(-1), TERMS)[1]
    shuffled = jax.random.permutation(key_order, chosen)
    leading = shuffled // SLOTS * NODE_DEV + jax.random.randint(key_local, (TERMS,), 0, NODE_DEV)
    second = (leading + 1 + jax.random.randint(key_other, (TERMS,), 0, NODES - 1)) % NODES
    return jnp.stack([leading, second], axis=1).astype(jnp.int32)


def set_ends(result, own_key, least, largest):
    longest = result.shape.index(max(result.shape))
    spots = []
    for shift in (0, 1):
        where = [jax.random.randint(jax.random.fold_in(own_key, axis), (), 0, length) for axis, length in enumerate(result.shape)]
        where[longest] = (where[longest] + shift) % result.shape[longest]
        spots.append(tuple(where))
    return result.at[spots[0]].set(least).at[spots[1]].set(largest)


def shard_levels(rng, dims, cuts, low, largest):
    gain, own = 1.0, jax.random.fold_in(rng, 6)
    for axis_at, shards_of in cuts:
        heights = jnp.exp(jax.random.uniform(jax.random.fold_in(own, axis_at), (shards_of,), jnp.float32, low / len(cuts), largest / len(cuts)))
        gain = gain * jnp.repeat(heights, dims[axis_at] // shards_of).reshape([-1 if axis == axis_at else 1 for axis in range(len(dims))])
    return gain


def centred(stream_key, shape, deviation, limit, cuts=(), kind=jnp.bfloat16):
    gain = shard_levels(stream_key, shape, cuts, -0.22, 0.18) if cuts else 1.0
    drawn = jax.random.normal(stream_key, shape, jnp.float32) * deviation * gain
    return jnp.minimum(jnp.maximum(drawn, -limit), limit).astype(kind)


def setup_inputs(seed: int = 0, part: int = 0) -> dict:
    key_of = jax.random.split(jax.random.key(seed), 5)
    part_splits = jax.random.split(jax.random.fold_in(key_of[4], part), 5)
    return {
        "meson_nodes": centred(part_splits[0], (2, NODES, ORDER, ORDER), 0.096, 0.66, ((1, 4), (2, 2), (3, 2)), jnp.float32),
        "term_nodes": draw_term_nodes(jax.random.fold_in(jax.random.fold_in(key_of[4], part), 71), part),
        "weight_codes": set_ends(jax.random.randint(part_splits[2], (TERMS,), 0, 8), jax.random.fold_in(part_splits[2], 1), 0, 7).astype(jnp.int32),
        "resident_pick": set_ends(jax.random.randint(part_splits[3], (NODES,), 0, NODE_DEV), jax.random.fold_in(part_splits[3], 1), 0, NODE_DEV - 1).astype(jnp.int32),
    }


def complex_product(left_matrix, right_matrix):
    highest = lax.Precision.HIGHEST
    real_part = jnp.dot(left_matrix[0], right_matrix[0], precision=highest, preferred_element_type=jnp.float32) - jnp.dot(left_matrix[1], right_matrix[1], precision=highest, preferred_element_type=jnp.float32)
    imag_part = jnp.dot(left_matrix[0], right_matrix[1], precision=highest, preferred_element_type=jnp.float32) + jnp.dot(left_matrix[1], right_matrix[0], precision=highest, preferred_element_type=jnp.float32)
    return jnp.stack([real_part, imag_part])


def reference(meson_nodes, term_nodes, weight_codes, resident_pick):
    factors = (weight_codes.astype(jnp.float32) - 3.5) * 0.5

    def one_term(pair_ids):
        return complex_product(meson_nodes[:, pair_ids[0]], meson_nodes[:, pair_ids[1]])

    products = lax.map(one_term, term_nodes)
    node_ids = jnp.arange(NODES, dtype=jnp.int32)
    incidence = (term_nodes[:, 0:1] == node_ids[None, :]).astype(jnp.float32) + (term_nodes[:, 1:2] == node_ids[None, :]).astype(jnp.float32)
    mixing = factors[:, None] * incidence
    summed = jnp.einsum("tn,tcij->cnij", mixing, products, precision=lax.Precision.HIGHEST)
    resident = (node_ids // NODE_DEV) * NODE_DEV + resident_pick

    def one_node(node_index):
        return complex_product(summed[:, node_index], meson_nodes[:, resident[node_index]])

    contracted = lax.map(one_node, node_ids)
    return jnp.transpose(contracted, (1, 0, 2, 3))
```

```python
import functools

import jax
import jax.numpy as jnp
from jax import lax
from jax.experimental import pallas as pl
from jax.experimental.pallas import tpu as pltpu
from jax.sharding import PartitionSpec as P


def complex_step(full_left, segment):
    highest = lax.Precision.HIGHEST
    real_part = jnp.einsum(
        "kij,kjl->kil",
        full_left[0],
        segment[0],
        precision=highest,
        preferred_element_type=jnp.float32,
    ) - jnp.einsum(
        "kij,kjl->kil",
        full_left[1],
        segment[1],
        precision=highest,
        preferred_element_type=jnp.float32,
    )
    imag_part = jnp.einsum(
        "kij,kjl->kil",
        full_left[0],
        segment[1],
        precision=highest,
        preferred_element_type=jnp.float32,
    ) + jnp.einsum(
        "kij,kjl->kil",
        full_left[1],
        segment[0],
        precision=highest,
        preferred_element_type=jnp.float32,
    )
    return jnp.stack([real_part, imag_part])


def wide_body(meson_nodes, term_nodes, weight_codes, resident_pick):
    node_count = lax.axis_size("node")
    owned = meson_nodes.shape[1]
    row_count = meson_nodes.shape[2]
    col_count = meson_nodes.shape[3]
    band = row_count // node_count
    total_nodes = owned * node_count
    term_count = term_nodes.shape[0]
    banded = meson_nodes.reshape(2, owned, node_count, band * col_count)
    spread = lax.all_to_all(banded, "node", split_axis=2, concat_axis=1, tiled=True).reshape(
        2, total_nodes, band * col_count
    )
    leading = term_nodes[:, 0]
    trailing = term_nodes[:, 1]
    worker_ids = jnp.arange(node_count, dtype=jnp.int32)
    slot_count = term_count // node_count
    table = jnp.arange(slot_count, dtype=jnp.int32)[None, :] * node_count + worker_ids[:, None]
    active = jnp.ones(table.shape, jnp.float32)
    first_table = leading[table]
    second_table = trailing[table]
    factors = active * (weight_codes[table].astype(jnp.float32) - 3.5) * 0.5
    wanted = jnp.stack([first_table.T, second_table.T], axis=1)
    picked = jnp.take(spread, wanted, axis=1)
    fetched = lax.all_to_all(picked, "node", split_axis=3, concat_axis=3, tiled=True).reshape(
        2, slot_count, 2, row_count, col_count
    )
    left_rows = fetched[:, :, 0]
    right_band = fetched[:, :, 1]
    left_full = lax.all_gather(left_rows, "rep", axis=3, tiled=True)
    products = complex_step(left_full, lax.all_gather(right_band, "sub", axis=2, tiled=True))
    outgoing = products.reshape(2, slot_count, node_count, band * col_count)
    returned = lax.all_to_all(outgoing, "node", split_axis=2, concat_axis=1, tiled=True).reshape(
        2, node_count * slot_count, band * col_count
    )
    node_ids = jnp.arange(total_nodes, dtype=jnp.int32)
    incidence = (first_table.reshape(-1)[:, None] == node_ids[None, :]).astype(jnp.float32) + (
        second_table.reshape(-1)[:, None] == node_ids[None, :]
    ).astype(jnp.float32)
    mixing = factors.reshape(-1)[:, None] * incidence
    summed = jnp.einsum("mn,cmx->cnx", mixing, returned, precision=lax.Precision.HIGHEST)
    owner_sum = lax.all_to_all(
        summed.reshape(2, total_nodes, 1, band * col_count),
        "node",
        split_axis=1,
        concat_axis=2,
        tiled=True,
    ).reshape(2, owned, row_count, col_count)
    sum_full = lax.all_gather(owner_sum, "rep", axis=3, tiled=True)
    own_index = lax.axis_index("node")
    picks = lax.dynamic_slice_in_dim(resident_pick, own_index * owned, owned)
    resident = jnp.take(meson_nodes, picks, axis=1)
    return complex_step(sum_full, lax.all_gather(resident, "sub", axis=2, tiled=True))


MESH = pl.DeviceIdType.MESH
PIECES = 4
FOREIGN = 2


def split(value):
    high = value.astype(jnp.bfloat16)
    return high, (value - high.astype(jnp.float32)).astype(jnp.bfloat16)


def mul(left, right):
    def dot(p, q):
        return jnp.dot(p, q, preferred_element_type=jnp.float32)

    return dot(left[0], right[0]) + (dot(left[0], right[1]) + dot(left[1], right[0]))


def complex_mul(a0, a1, b0, b1):
    left, right = split(a0), split(b0)
    both = mul(left, right)
    left, right = split(a1), split(b1)
    other = mul(left, right)
    cross = mul(split(a0 + a1), split(b0 + b1))
    return both - other, cross - both - other


def line_kernel(
    length, owned, terms,
    x_ref, tn_ref, wc_ref, rp_ref, out_ref,
    nodes, rows, others, sums, picked,
    loc_sem, z_send, z_recv, c_send, c_recv, x_send, x_recv, s_send, s_recv,
):
    z = lax.axis_index("node")
    x = lax.axis_index("sub")
    c = lax.axis_index("rep")
    g = lax.axis_index("grp")
    left = (g, z - 1, x, c)
    right = (g, z + 1, x, c)
    across = (g, z, 1 - x, c)
    twin = (g, z, x, 1 - c)
    has_left = z > 0
    has_right = z < length - 1
    height = x_ref.shape[2] // PIECES
    pieces = [(j, m, r) for j in range(owned) for m in range(2) for r in range(PIECES)]

    def band(r):
        return pl.ds(r * height, height)

    def remote(src, dst, send, recv, device):
        return pltpu.make_async_remote_copy(
            src_ref=src, dst_ref=dst, send_sem=send, recv_sem=recv, device_id=device, device_id_type=MESH
        )

    barrier = pltpu.get_barrier_semaphore()
    for device in (across, twin):
        pl.semaphore_signal(barrier, inc=1, device_id=device, device_id_type=MESH)

    @pl.when(has_left)
    def _():
        pl.semaphore_signal(barrier, inc=1, device_id=left, device_id_type=MESH)

    @pl.when(has_right)
    def _():
        pl.semaphore_signal(barrier, inc=1, device_id=right, device_id_type=MESH)

    pl.semaphore_wait(barrier, 2 + has_left.astype(jnp.int32) + has_right.astype(jnp.int32))

    def node_at(owner, j, m, r):
        return nodes.at[c, owner * owned + j, m, band(r)]

    def own_at(j, m, r):
        return x_ref.at[m, j, band(r)]

    def reach(way, step):
        return z + step if way == 0 else z - step

    def inside(owner):
        return jnp.logical_and(owner >= 0, owner <= length - 1)

    def to_end(way):
        return z == (1 if way == 0 else length - 2)

    def z_sends(way, step):
        found = jnp.logical_and(has_left if way == 0 else has_right, inside(reach(way, step)))
        return jnp.logical_and(found, jnp.logical_not(to_end(way))) if step == 0 else found

    def z_arrives(way, step):
        found = inside(reach(way, step + 1))
        return jnp.logical_and(found, z != (0 if way == 0 else length - 1)) if step == 0 else found

    def z_copy(way, step, j, m, r, src):
        return remote(
            src, node_at(reach(way, step), j, m, r), z_send.at[way, step, j, m, r],
            z_recv.at[way, step, j, m, r], left if way == 0 else right,
        )

    def c_copy(owner, j, m, r, src):
        return remote(
            src, node_at(owner, j, m, r), c_send.at[owner, j, m, r], c_recv.at[owner, j, m, r], twin
        )

    def x_copy(k, m, r, src):
        return remote(src, others.at[k, m, band(r)], x_send.at[k, m, r], x_recv.at[k, m, r], across)

    def s_copy(h, j, m):
        return remote(sums.at[h, j, m], sums.at[h, j, m], s_send.at[j, m], s_recv.at[j, m], twin)

    for way in range(2):

        @pl.when(z_sends(way, 0))
        def _():
            for piece in pieces:
                z_copy(way, 0, *piece, own_at(*piece)).start()

    for piece in pieces:
        x_copy(*piece, own_at(*piece)).start()
    local = []
    for j, m, r in pieces:
        for i, dst in enumerate((node_at(z, j, m, r), rows.at[j, m, band(r)])):
            copy = pltpu.make_async_copy(own_at(j, m, r), dst, loc_sem.at[i, j, m, r])
            copy.start()
            local.append(copy)
        c_copy(z, j, m, r, own_at(j, m, r)).start()

    firsts = [tn_ref[0, t] for t in range(terms)]
    seconds = [tn_ref[1, t] for t in range(terms)]
    spots = (length - 2) * owned

    def holds(owner, n):
        return jnp.logical_and(n >= owner * owned, n < owner * owned + owned)

    def rank_of(end, n):
        owner = n // owned
        return jnp.where(end == 0, owner, length - 1 - owner) * owned + n - owner * owned

    def node_of(end, rank):
        far = rank // owned
        return jnp.where(end == 0, far, length - 1 - far) * owned + rank % owned

    def partner_ranks(end):
        ranks = []
        for a, b in zip(firsts, seconds):
            here, there = holds(end, a), holds(end, b)
            rank = jnp.where(here, rank_of(end, b), rank_of(end, a))
            ranks.append(jnp.where(here != there, rank, owned))
        below, found = length * owned, []
        for _ in range(spots):
            best = owned
            for rank in ranks:
                best = jnp.where(jnp.logical_and(rank < below, rank > best), rank, best)
            found.append(best)
            below = best
        return found[::-1]

    end = jnp.where(z < length // 2, 0, length - 1)
    wanted_ranks = partner_ranks(end)
    at_end = z == end

    def entry(n):
        place = z * owned
        rank = rank_of(end, n)
        for i in range(spots):
            place = jnp.where(wanted_ranks[i] == rank, node_of(end, 2 * owned + i), place)
        return jnp.where(jnp.logical_and(at_end, jnp.logical_not(holds(z, n))), place, n)

    far = length - 1 - end
    late = far * owned + owned - 1
    home = z * owned
    left_entries = [entry(a) for a in firsts]
    right_entries = [entry(b) for b in seconds]
    needs = [
        jnp.logical_and(holds(z, a), jnp.logical_not(holds(z, b))) for a, b in zip(firsts, seconds)
    ]
    slot1 = home
    for need, e in zip(needs, right_entries):
        slot1 = jnp.where(jnp.logical_and(need, slot1 != late), e, slot1)
    slot0 = home
    for need, e in zip(needs, right_entries):
        slot0 = jnp.where(jnp.logical_and(need, e != slot1), e, slot0)

    for copy in local:
        copy.wait()

    def pick(i, m, r):
        chosen = nodes[c, node_of(end, owned), m, band(r)]
        for rank in range(owned + 1, 2 * owned + i + 1):
            chosen = jnp.where(
                wanted_ranks[i] == rank, nodes[c, node_of(end, rank), m, band(r)], chosen
            )
        picked[i, m, band(r)] = chosen

    def stage(s, m, r):
        wanted = slot1 if s else slot0
        chosen = nodes[c, home, m, band(r)]
        for k in range(length):
            owner = lax.rem(far + 1 + k, length)
            for j in range(owned):
                if s == 0 and k == length - 1 and j == owned - 1:
                    continue
                n = owner * owned + j
                chosen = jnp.where(wanted == n, nodes[c, n, m, band(r)], chosen)
        rows[owned + s, m, band(r)] = chosen
        x_copy(owned + s, m, r, rows.at[owned + s, m, band(r)]).start()

    depth = jnp.maximum(z, length - 1 - z) - 1
    for step in range(length - 1):
        for j, m, r in pieces:
            for way in range(2):

                @pl.when(z_arrives(way, step))
                def _():
                    owner = reach(way, step + 1)
                    src = node_at(owner, j, m, r)
                    remote(
                        src, src, z_send.at[way, step, j, m, r], z_recv.at[way, step, j, m, r],
                        left if way == 0 else right,
                    ).wait_recv()
                    c_copy(owner, j, m, r, src).start()

                if step < length - 2:
                    goes = jnp.logical_and(z_arrives(way, step), z_sends(way, step + 1))

                    @pl.when(jnp.logical_and(goes, jnp.logical_not(to_end(way))))
                    def _():
                        z_copy(way, step + 1, j, m, r, node_at(reach(way, step + 1), j, m, r)).start()

                    @pl.when(jnp.logical_and(goes, to_end(way)))
                    def _():
                        i = step * owned + j
                        pick(i, m, r)
                        z_copy(way, step + 1, j, m, r, picked.at[i, m, band(r)]).start()

            if step >= length // 2 - 1:

                @pl.when(depth == step)
                def _():
                    stage(j, m, r)

    def filled(owner):
        beside = jnp.where(end == 0, 1, length - 2)
        return jnp.logical_not(jnp.logical_and(at_end, owner == beside))

    for owner in range(length):

        @pl.when(filled(owner))
        def _():
            for j, m, r in pieces:
                dst = nodes.at[1 - c, owner * owned + j, m, band(r)]
                remote(dst, dst, c_send.at[owner, j, m, r], c_recv.at[owner, j, m, r], twin).wait_recv()

    def products(h, held, fresh):
        for t in range(terms):
            a, b = firsts[t], seconds[t]
            e, f = left_entries[t], right_entries[t]
            k = jnp.where(holds(z, b), b - home, jnp.where(f == slot1, owned + 1, owned))
            parts = complex_mul(nodes[h, e, 0], nodes[h, e, 1], held[k, 0], held[k, 1])
            factor = (wc_ref[t].astype(jnp.float32) - 3.5) * 0.5
            for j in range(owned):
                n = home + j
                count = (a == n).astype(jnp.float32) + (b == n).astype(jnp.float32)
                weight = factor * count
                for m in range(2):
                    if t == 0 and fresh:
                        sums[c, j, m] = weight * parts[m]
                    else:
                        sums[c, j, m] = sums[c, j, m] + weight * parts[m]

    products(x, rows, True)
    for k in range(owned + FOREIGN):
        for m in range(2):
            for r in range(PIECES):
                dst = others.at[k, m, band(r)]
                remote(dst, dst, x_send.at[k, m, r], x_recv.at[k, m, r], across).wait_recv()
    products(1 - x, others, False)

    for j in range(owned):
        for m in range(2):
            s_copy(c, j, m).start()
    for h in (c, 1 - c):
        for j in range(owned):
            if h is not c:
                for m in range(2):
                    s_copy(h, j, m).wait_recv()
            choice = rp_ref[home + j]
            here = [jnp.where(h == x, rows[choice, m], others[choice, m]) for m in range(2)]
            parts = complex_mul(sums[h, j, 0], sums[h, j, 1], here[0], here[1])
            for m in range(2):
                out_ref[m, j] = parts[m] if h is c else out_ref[m, j] + parts[m]

    for j in range(owned):
        for m in range(2):
            s_copy(c, j, m).wait_send()
    for piece in pieces:
        x_copy(*piece, own_at(*piece)).wait_send()
    for s in range(FOREIGN):
        for m in range(2):
            for r in range(PIECES):
                x_copy(owned + s, m, r, rows.at[owned + s, m, band(r)]).wait_send()
    for step in range(length - 1):
        for way in range(2):

            @pl.when(z_sends(way, step))
            def _():
                for piece in pieces:
                    z_copy(way, step, *piece, own_at(*piece)).wait_send()

    for owner in range(length):

        @pl.when(filled(owner))
        def _():
            for piece in pieces:
                c_copy(owner, *piece, own_at(*piece)).wait_send()


def line_body(meson_nodes, term_nodes, weight_codes, resident_pick):
    length = lax.axis_size("node")
    _, owned, height, width = meson_nodes.shape
    terms = term_nodes.shape[0]
    block = (height, width)
    vmem = pl.BlockSpec(memory_space=pltpu.VMEM)
    smem = pl.BlockSpec(memory_space=pltpu.SMEM)
    dma = pltpu.SemaphoreType.DMA
    slots = owned + FOREIGN
    return pl.pallas_call(
        functools.partial(line_kernel, length, owned, terms),
        out_shape=pltpu.VMEM(meson_nodes.shape, jnp.float32),
        in_specs=[pl.BlockSpec(memory_space=pl.ANY), smem, smem, smem],
        out_specs=vmem,
        scratch_shapes=[
            pltpu.VMEM((2, length * owned, 2) + block, jnp.float32),
            pltpu.VMEM((slots, 2) + block, jnp.float32),
            pltpu.VMEM((slots, 2) + block, jnp.float32),
            pltpu.VMEM((2, owned, 2) + block, jnp.float32),
            pltpu.VMEM(((length - 2) * owned, 2) + block, jnp.float32),
            dma((2, owned, 2, PIECES)),
            dma((2, length - 1, owned, 2, PIECES)),
            dma((2, length - 1, owned, 2, PIECES)),
            dma((length, owned, 2, PIECES)),
            dma((length, owned, 2, PIECES)),
            dma((slots, 2, PIECES)),
            dma((slots, 2, PIECES)),
            dma((owned, 2)),
            dma((owned, 2)),
        ],
        compiler_params=pltpu.CompilerParams(
            collective_id=0, has_side_effects=True, vmem_limit_bytes=58 << 20
        ),
    )(meson_nodes, term_nodes.T, weight_codes, resident_pick)


def body(meson_nodes, term_nodes, weight_codes, resident_pick):
    length, owned = lax.axis_size("node"), meson_nodes.shape[1]
    square = meson_nodes.shape[2] == meson_nodes.shape[3]
    halves = lax.axis_size("sub") == 2 and lax.axis_size("rep") == 2
    held = 2 * length * meson_nodes.size * 4
    fits = held <= 16 << 20 and term_nodes.shape[0] <= (length - 2) * owned
    if square and halves and fits and owned == FOREIGN and length == 4:
        return line_body(meson_nodes, term_nodes, weight_codes, resident_pick)
    return wide_body(meson_nodes, term_nodes, weight_codes, resident_pick)


def solution(mesh):
    in_specs = (P(None, ("grp", "node"), "sub", "rep"), P("grp", None), P("grp"), P("grp"))
    out_specs = P(None, ("grp", "node"), "sub", "rep")
    return jax.shard_map(body, mesh=mesh, in_specs=in_specs, out_specs=out_specs, check_vma=False)
```

```python
import functools

import jax
import jax.numpy as jnp
from jax import lax
from jax.experimental import pallas as pl
from jax.experimental.pallas import tpu as pltpu
from jax.sharding import PartitionSpec as P


def complex_step(full_left, segment):
    highest = lax.Precision.HIGHEST
    real_part = jnp.einsum(
        "kij,kjl->kil",
        full_left[0],
        segment[0],
        precision=highest,
        preferred_element_type=jnp.float32,
    ) - jnp.einsum(
        "kij,kjl->kil",
        full_left[1],
        segment[1],
        precision=highest,
        preferred_element_type=jnp.float32,
    )
    imag_part = jnp.einsum(
        "kij,kjl->kil",
        full_left[0],
        segment[1],
        precision=highest,
        preferred_element_type=jnp.float32,
    ) + jnp.einsum(
        "kij,kjl->kil",
        full_left[1],
        segment[0],
        precision=highest,
        preferred_element_type=jnp.float32,
    )
    return jnp.stack([real_part, imag_part])


def wide_body(meson_nodes, term_nodes, weight_codes, resident_pick):
    node_count = lax.axis_size("node")
    owned = meson_nodes.shape[1]
    row_count = meson_nodes.shape[2]
    col_count = meson_nodes.shape[3]
    band = row_count // node_count
    total_nodes = owned * node_count
    term_count = term_nodes.shape[0]
    banded = meson_nodes.reshape(2, owned, node_count, band * col_count)
    spread = lax.all_to_all(banded, "node", split_axis=2, concat_axis=1, tiled=True).reshape(
        2, total_nodes, band * col_count
    )
    leading = term_nodes[:, 0]
    trailing = term_nodes[:, 1]
    worker_ids = jnp.arange(node_count, dtype=jnp.int32)
    slot_count = term_count // node_count
    table = jnp.arange(slot_count, dtype=jnp.int32)[None, :] * node_count + worker_ids[:, None]
    active = jnp.ones(table.shape, jnp.float32)
    first_table = leading[table]
    second_table = trailing[table]
    factors = active * (weight_codes[table].astype(jnp.float32) - 3.5) * 0.5
    wanted = jnp.stack([first_table.T, second_table.T], axis=1)
    picked = jnp.take(spread, wanted, axis=1)
    fetched = lax.all_to_all(picked, "node", split_axis=3, concat_axis=3, tiled=True).reshape(
        2, slot_count, 2, row_count, col_count
    )
    left_rows = fetched[:, :, 0]
    right_band = fetched[:, :, 1]
    left_full = lax.all_gather(left_rows, "rep", axis=3, tiled=True)
    products = complex_step(left_full, lax.all_gather(right_band, "sub", axis=2, tiled=True))
    outgoing = products.reshape(2, slot_count, node_count, band * col_count)
    returned = lax.all_to_all(outgoing, "node", split_axis=2, concat_axis=1, tiled=True).reshape(
        2, node_count * slot_count, band * col_count
    )
    node_ids = jnp.arange(total_nodes, dtype=jnp.int32)
    incidence = (first_table.reshape(-1)[:, None] == node_ids[None, :]).astype(jnp.float32) + (
        second_table.reshape(-1)[:, None] == node_ids[None, :]
    ).astype(jnp.float32)
    mixing = factors.reshape(-1)[:, None] * incidence
    summed = jnp.einsum("mn,cmx->cnx", mixing, returned, precision=lax.Precision.HIGHEST)
    owner_sum = lax.all_to_all(
        summed.reshape(2, total_nodes, 1, band * col_count),
        "node",
        split_axis=1,
        concat_axis=2,
        tiled=True,
    ).reshape(2, owned, row_count, col_count)
    sum_full = lax.all_gather(owner_sum, "rep", axis=3, tiled=True)
    own_index = lax.axis_index("node")
    picks = lax.dynamic_slice_in_dim(resident_pick, own_index * owned, owned)
    resident = jnp.take(meson_nodes, picks, axis=1)
    return complex_step(sum_full, lax.all_gather(resident, "sub", axis=2, tiled=True))


MESH = pl.DeviceIdType.MESH
UNITS = (2,) * 15 + (1, 1)
LEADS = (4, 3, 3, 2, 2)
BATCHES = (2,) * 6 + (1,) * 5
GROUPS = 4


def split(value):
    high = value.astype(jnp.bfloat16)
    return high, (value - high.astype(jnp.float32)).astype(jnp.bfloat16)


def dot(p, q):
    return jnp.dot(p, q, preferred_element_type=jnp.float32)


def stacked_mul(l0, l1, right):
    rows = l0.shape[0]
    a, b = split(l0)
    c, d = split(l1)
    four = jnp.concatenate([a, b, c, d], axis=0)
    two = jnp.concatenate([a, c], axis=0)
    by_real, by_imag = dot(four, right(0)), dot(four, right(2))
    low_real, low_imag = dot(two, right(1)), dot(two, right(3))

    def part(value, i):
        return value[i * rows : (i + 1) * rows]

    def product(high, low, i):
        return part(high, 2 * i) + (part(high, 2 * i + 1) + part(low, i))

    real = product(by_real, low_real, 0) - product(by_imag, low_imag, 1)
    imag = product(by_imag, low_imag, 0) + product(by_real, low_real, 1)
    return real, imag


def sliced_mul(left, r0, r1):
    def mul(i, value):
        high, low = split(value)
        return dot(left(i), high) + (dot(left(i), low) + dot(left(i + 1), high))

    both, other, cross = mul(0, r0), mul(2, r1), mul(4, r0 + r1)
    return both - other, cross - both - other


def packed_mul(left, r0, r1):
    def mul(i, value):
        high, low = split(value)
        return dot(left(i), jnp.concatenate([high, high, low], axis=0))

    both, other, cross = mul(0, r0), mul(1, r1), mul(2, r0 + r1)
    return both - other, cross - both - other


def pieces_of(height):
    unit = height // sum(UNITS)
    pieces, at = [], 0
    for size in UNITS:
        pieces.append((at, size * unit))
        at += size * unit
    return pieces


def arrivals_of(pieces):
    order, sent = [], 0
    for r in range(len(pieces)):
        lead = LEADS[r] if r < len(LEADS) else 1 + (r >= len(pieces) - 2)
        while sent < min(r + lead, len(pieces)):
            order.append((0, sent))
            sent += 1
        order.append((1, r))
    return order


def plan_of(order, pieces, height):
    after = {
        (0, 1): [("pass", 1), ("right", 0), ("right", 1), ("right", 2), ("right", 3), ("left", 0)],
        (0, 2): [("pass", 3), ("left", 1)],
        (1, 0): [("pass", 5), ("facing", 0)],
        (0, 4): [("pass", 7)],
        (1, 3): [("pass", 9), ("facing", 1)],
        (1, 4): [("pass", 11)],
        (1, 5): [("facing", 2)],
        (0, 6): [("pass", 13)],
        (1, 7): [("facing", 3), ("turn", 0)],
        (0, 8): [("pass", 16), ("turn", 1), ("turn", 2)],
        (1, 8): [("turn", 3), ("up", 0)],
        (0, 9): [("up", 1)],
        (1, 9): [("down", 0)],
        (0, 10): [("turn", 4), ("down", 1)],
        (1, 10): [("mine", 0)],
        (0, 12): [("turn", 5), ("up", 2)],
        (0, 13): [("turn", 6), ("down", 2)],
        (1, 13): [("theirs", 0)],
        (0, 14): [("turn", 7), ("mine", 1)],
        (1, 14): [("up", 3)],
        (0, 16): [("turn", 8)],
        (1, 15): [("theirs", 1)],
        (1, 16): [("turn", 9), ("turn", 10), ("up", 4), ("down", 3), ("mine", 2), ("down", 4), ("theirs", 2)],
    }
    plan = []
    for kind, r in order:
        plan.append(("far" if kind else "near", r))
        plan += after.get((kind, r), [])
    return plan


def line_kernel(
    length, owned, terms,
    x_ref, tn_ref, wc_ref, rp_ref, out_ref,
    own, beside, facing, outer, inner, far, near_pick, far_pick,
    mixes, turned, turned_far, lefts, packs, rights, ups,
    loc_sem, z_send, z_recv, o_recv, x_send, x_recv, t_recv, c_send, c_recv, m_recv, u_recv, ready,
):
    z = lax.axis_index("node")
    x = lax.axis_index("sub")
    c = lax.axis_index("rep")
    g = lax.axis_index("grp")
    above = (g, z + 1, x, c)
    below = (g, z - 1, x, c)
    across = (g, z, 1 - x, c)
    twin = (g, z, x, 1 - c)
    height = x_ref.shape[2]
    pieces = pieces_of(height)
    count = len(pieces)
    order = arrivals_of(pieces)
    group = height // GROUPS
    groups = [(at, group) for at in range(0, height, group)]
    slices = [(0, 2 * group), (2 * group, group), (3 * group, group)]
    lifts = groups[:3] + [(3 * group, group // 2), (3 * group + group // 2, group // 2)]
    batches, first = [], 0
    for size in BATCHES:
        batches.append((pieces[first][0], sum(tall for _, tall in pieces[first : first + size])))
        first += size
    closing = {sum(BATCHES[: k + 1]) - 1: k for k in range(len(BATCHES))}
    raws = [(at, group // 2) for at in range(0, height, group // 2)]
    low = z < length // 2
    is_end = jnp.logical_or(z == 0, z == length - 1)
    is_mid = jnp.logical_not(is_end)
    end = jnp.where(low, 0, length - 1)
    far_end = length - 1 - end
    toward_end = (g, jnp.where(low, z - 1, z + 1), x, c)
    toward_mid = (g, jnp.where(low, z + 1, z - 1), x, c)

    def remote(src, dst, send, recv, device):
        return pltpu.make_async_remote_copy(
            src_ref=src, dst_ref=dst, send_sem=send, recv_sem=recv, device_id=device, device_id_type=MESH
        )

    def rows(r):
        return pl.ds(*pieces[r])

    def raw_copy(k):
        span = pl.ds(*raws[k])
        return remote(
            x_ref.at[:, :, span], outer.at[:, :, span], z_send.at[0], o_recv.at[k], toward_mid
        )

    def own_copy(r):
        return remote(
            x_ref.at[:, :, rows(r)], inner.at[:, :, rows(r)], z_send.at[1], z_recv.at[0, r], toward_mid
        )

    def pass_copy(r):
        return remote(
            outer.at[:, :, rows(r)], far.at[:, :, rows(r)], z_send.at[2], z_recv.at[1, r], toward_mid
        )

    def near_copy(r):
        return remote(
            near_pick.at[:, :, rows(r)], inner.at[:, :, rows(r)], z_send.at[3], z_recv.at[0, r], toward_end
        )

    def far_copy(r):
        return remote(
            far_pick.at[:, :, rows(r)], far.at[:, :, rows(r)], z_send.at[4], z_recv.at[1, r], toward_end
        )

    def x_copy(k):
        span = pl.ds(*groups[k])
        return remote(
            x_ref.at[:, :, span], facing.at[:, :, span], x_send.at[0], x_recv.at[k], across
        )

    def turned_copy(k):
        span = pl.ds(*batches[k])
        return remote(
            turned.at[:, :, span], turned_far.at[:, :, span], x_send.at[1], t_recv.at[k], across
        )

    def c_copy(j):
        return remote(x_ref.at[:, j], beside.at[:, j], c_send.at[0], c_recv.at[j], twin)

    def mix_copy(slot, k):
        part = mixes.at[slot, :, :, pl.ds(*batches[k])]
        return remote(part, part, c_send.at[1], m_recv.at[k], twin)

    def up_copy(slot, k):
        part = ups.at[slot, :, :, pl.ds(*lifts[k])]
        return remote(part, part, c_send.at[2], u_recv.at[k], twin)

    barrier = pltpu.get_barrier_semaphore()
    ENTER = ((z < length - 1, above, z > 0, below), (x == 0, across, x == 1, across), (c == 1, twin, c == 0, twin))
    waits = 0
    for early, later_device, late, _ in ENTER:

        @pl.when(early)
        def _():
            pl.semaphore_signal(barrier, inc=1, device_id=later_device, device_id_type=MESH)

        waits = waits + late.astype(jnp.int32)

    @pl.when(waits > 0)
    def _():
        pl.semaphore_wait(barrier, waits)

    for i, (_, _, late, early_device) in enumerate(ENTER):

        @pl.when(late)
        def _():
            pl.semaphore_signal(ready.at[i], inc=1, device_id=early_device, device_id_type=MESH)

    def meet(i):
        @pl.when(ENTER[i][0])
        def _():
            pl.semaphore_wait(ready.at[i], 1)

    first_own = order[: order.index((1, 0))]
    passing = {"sent": len(first_own), "raw": 0}

    def send_until(r):
        last = order.index((1, r)) + 1

        @pl.when(is_mid)
        def _():
            for kind, p in order[passing["sent"] : last]:
                if kind == 0:
                    own_copy(p).start()
                else:
                    while raws[passing["raw"] - 1][0] + raws[0][1] < sum(pieces[p]) or passing["raw"] == 0:
                        raw_copy(passing["raw"]).wait_recv()
                        passing["raw"] += 1
                    pass_copy(p).start()

        passing["sent"] = last

    def open_sends():
        @pl.when(is_end)
        def _():
            for k in range(len(raws)):
                raw_copy(k).start()

        @pl.when(is_mid)
        def _():
            for _, p in first_own:
                own_copy(p).start()

    @pl.when(jnp.logical_not(low))
    def _():
        open_sends()

    meet(0)

    @pl.when(low)
    def _():
        open_sends()

    meet(2)
    for j in range(owned):
        c_copy(j).start()
    local = pltpu.make_async_copy(x_ref, own, loc_sem.at[0])
    local.start()
    meet(1)
    for k in range(GROUPS):
        x_copy(k).start()

    firsts = [tn_ref[0, t] for t in range(terms)]
    seconds = [tn_ref[1, t] for t in range(terms)]
    factors = [(wc_ref[t].astype(jnp.float32) - 3.5) * 0.5 for t in range(terms)]
    choices = [rp_ref[z * owned + n] for n in range(owned)]
    spots = (length - 2) * owned

    def holds(owner, n):
        return jnp.logical_and(n >= owner * owned, n < owner * owned + owned)

    def rank_of(n):
        owner = n // owned
        return jnp.where(end == 0, owner, length - 1 - owner) * owned + n - owner * owned

    def node_of(rank):
        far_owner = rank // owned
        return jnp.where(end == 0, far_owner, length - 1 - far_owner) * owned + rank % owned

    def partner_ranks():
        ranks = []
        for a, b in zip(firsts, seconds):
            here, there = holds(end, a), holds(end, b)
            rank = jnp.where(here, rank_of(b), rank_of(a))
            ranks.append(jnp.where(here != there, rank, owned))
        below_rank, found = length * owned, []
        for _ in range(spots):
            best = owned
            for rank in ranks:
                best = jnp.where(jnp.logical_and(rank < below_rank, rank > best), rank, best)
            found.append(best)
            below_rank = best
        return found[::-1]

    wanted = partner_ranks()
    spot_nodes = []
    for i in range(spots):
        node = node_of(wanted[i])
        if i < spots - 1:
            node = jnp.where(wanted[i] == wanted[i + 1], -1, node)
        spot_nodes.append(node)
    home = z * owned
    near_mid = jnp.where(low, z + 1, z - 1) * owned
    entry_nodes = [home + j for j in range(owned)]
    entry_nodes += [jnp.where(is_mid, near_mid + j, spot_nodes[j]) for j in range(owned)]
    entry_nodes += [jnp.where(is_mid, far_end * owned + j, spot_nodes[owned + j]) for j in range(owned)]
    entry_nodes += [end * owned + j for j in range(owned)]
    zero = jnp.float32(0)

    def weight_of(keys, partners, n, node):
        total = zero
        for t in range(terms):
            match = jnp.logical_and(keys[t] == n, partners[t] == node)
            total = total + jnp.where(match, factors[t], zero)
        return total

    weights = [
        [weight_of(keys, partners, home + n, node) for node in entry_nodes]
        for keys, partners in ((seconds, firsts), (firsts, seconds))
        for n in range(owned)
    ]

    def blend(r, whole):
        for m in range(2):
            held = [ref[m, j, rows(r)] for ref in (own, inner, far) for j in range(owned)]
            if whole:
                held += [outer[m, j, rows(r)] for j in range(owned)]
            for q, row in enumerate(weights):
                total = row[0] * held[0]
                for value, part in zip(row[1:], held[1:]):
                    total = total + value * part
                mixes[c, q, m, rows(r)] = total

    def pick(dst, i, spot, r, sources):
        for m in range(2):
            chosen = sources[0][0][m, sources[0][1], rows(r)]
            for k, (ref, j) in enumerate(sources[1:]):
                chosen = jnp.where(wanted[spot] == owned + 1 + k, ref[m, j, rows(r)], chosen)
            dst[m, i, rows(r)] = chosen

    ranked = [(ref, j) for ref in (own, inner, far) for j in range(owned)]

    def arrive(kind, r):
        @pl.when(is_mid)
        def _():
            if kind == 0:
                own_copy(r).wait_recv()
                for i in range(owned):
                    pick(near_pick, i, i, r, ranked[: owned + 1 + i])
                near_copy(r).start()
            else:
                pass_copy(r).wait_recv()
                for i in range(owned):
                    pick(far_pick, i, owned + i, r, ranked[: 2 * owned + 1 + i])
                far_copy(r).start()
                blend(r, True)

        @pl.when(is_end)
        def _():
            if kind == 0:
                near_copy(r).wait_recv()
            else:
                far_copy(r).wait_recv()
                blend(r, False)

        if kind == 1 and r in closing:
            mix_copy(c, closing[r]).start()

    def clear():
        out_ref[...] = jnp.zeros_like(out_ref)

    def put_right(ref, h, k):
        span = pl.ds(*groups[k])
        for j in range(owned):
            for m in range(2):
                for i, part in enumerate(split(ref[m, j, span])):
                    rights[j, 2 * m + i, h, span] = part

    def put_left(ref, h, n):
        re, im = ref[0, n], ref[1, n]
        for k, value in enumerate((re, im, re + im)):
            high, low_part = split(value)
            at, size = slices[0]
            lefts[n, 2 * k, h] = high[:, at : at + size]
            lefts[n, 2 * k + 1, h] = low_part[:, at : at + size]
            for i, (at, size) in enumerate(slices[1:]):
                part = high[:, at : at + size]
                packs[n, k, h, i] = jnp.concatenate([part, low_part[:, at : at + size], part], axis=1)

    def prepare_facing(k):
        x_copy(k).wait_recv()
        put_right(facing, 1 - x, k)

    def prepare_left(n):
        put_left(own, c, n)
        c_copy(n).wait_recv()
        put_left(beside, 1 - c, n)

    def right_of(n):
        return lambda i: rights[n, i].reshape(2 * height, height)

    def wide(ref, q, m, span):
        return jnp.concatenate([ref[h, q, m, span] for h in range(2)], axis=1)

    def turn(k):
        mix_copy(1 - c, k).wait_recv()
        span = pl.ds(*batches[k])
        for n in range(owned):
            q = owned + n
            parts = stacked_mul(wide(mixes, q, 0, span), wide(mixes, q, 1, span), right_of(choices[n]))
            for m in range(2):
                turned[n, m, span] = parts[m]
        turned_copy(k).start()

    def raise_up(k):
        span = pl.ds(*lifts[k])
        for n in range(owned):
            parts = stacked_mul(wide(mixes, n, 0, span), wide(mixes, n, 1, span), right_of(n))
            for m in range(2):
                ups[c, n, m, span] = parts[m]
        up_copy(c, k).start()

    def finish_up(k):
        up_copy(1 - c, k).wait_recv()
        span = pl.ds(*lifts[k])
        for n in range(owned):
            parts = stacked_mul(wide(ups, n, 0, span), wide(ups, n, 1, span), right_of(choices[n]))
            for m in range(2):
                out_ref[m, n, span] = out_ref[m, n, span] + parts[m]

    def add_slice(ref, h, k):
        at, size = slices[k]
        for n in range(owned):
            r0, r1 = ref[n, 0, at : at + size], ref[n, 1, at : at + size]
            if k == 0:
                parts = sliced_mul(lambda i: lefts[n, i, h], r0, r1)
            else:
                parts = packed_mul(lambda i: packs[n, i, h, k - 1], r0, r1)
            for m in range(2):
                out_ref[m, n] = out_ref[m, n] + parts[m]

    def add_theirs(k):
        at, size = slices[k]
        for i, (start, _) in enumerate(batches):
            if at <= start < at + size:
                turned_copy(i).wait_recv()
        add_slice(turned_far, 1 - x, k)

    clear()
    local.wait()

    plan = plan_of(order, pieces, height)
    actions = {
        "pass": send_until,
        "near": lambda r: arrive(0, r),
        "far": lambda r: arrive(1, r),
        "right": lambda k: put_right(own, x, k),
        "left": prepare_left,
        "facing": prepare_facing,
        "turn": turn,
        "up": raise_up,
        "down": finish_up,
        "mine": lambda k: add_slice(turned, x, k),
        "theirs": add_theirs,
    }
    for name, i in plan:
        with jax.named_scope(f"{name}{i}"):
            actions[name](i)

    remote(x_ref, facing, x_send.at[0], x_recv.at[0], across).wait_send()
    remote(turned, turned_far, x_send.at[1], t_recv.at[0], across).wait_send()
    remote(x_ref, beside, c_send.at[0], c_recv.at[0], twin).wait_send()
    remote(mixes.at[c], mixes.at[c], c_send.at[1], m_recv.at[0], twin).wait_send()
    remote(ups.at[c], ups.at[c], c_send.at[2], u_recv.at[0], twin).wait_send()

    @pl.when(is_end)
    def _():
        remote(x_ref, outer, z_send.at[0], o_recv.at[0], toward_mid).wait_send()

    @pl.when(is_mid)
    def _():
        remote(x_ref, inner, z_send.at[1], z_recv.at[0, 0], toward_mid).wait_send()
        remote(outer, far, z_send.at[2], z_recv.at[1, 0], toward_mid).wait_send()
        remote(near_pick, inner, z_send.at[3], z_recv.at[0, 0], toward_end).wait_send()
        remote(far_pick, far, z_send.at[4], z_recv.at[1, 0], toward_end).wait_send()


def line_body(meson_nodes, term_nodes, weight_codes, resident_pick):
    length = lax.axis_size("node")
    _, owned, height, width = meson_nodes.shape
    terms = term_nodes.shape[0]
    block = (height, width)
    vmem = pl.BlockSpec(memory_space=pltpu.VMEM)
    smem = pl.BlockSpec(memory_space=pltpu.SMEM)
    dma = pltpu.SemaphoreType.DMA
    count = len(UNITS)
    whole = pltpu.VMEM((2, owned) + block, jnp.float32)
    return pl.pallas_call(
        functools.partial(line_kernel, length, owned, terms),
        out_shape=pltpu.VMEM(meson_nodes.shape, jnp.float32),
        in_specs=[pl.BlockSpec(memory_space=pl.ANY), smem, smem, smem],
        out_specs=vmem,
        scratch_shapes=[whole] * 8
        + [
            pltpu.VMEM((2, 2 * owned, 2) + block, jnp.float32),
            pltpu.VMEM((owned, 2) + block, jnp.float32),
            pltpu.VMEM((owned, 2) + block, jnp.float32),
            pltpu.VMEM((owned, 6, 2, height, width // 2), jnp.bfloat16),
            pltpu.VMEM((owned, 3, 2, 2, height, 3 * width // GROUPS), jnp.bfloat16),
            pltpu.VMEM((owned, 4, 2) + block, jnp.bfloat16),
            pltpu.VMEM((2, owned, 2) + block, jnp.float32),
            dma((1,)),
            dma((5,)),
            dma((2, count)),
            dma((2 * GROUPS,)),
            dma((2,)),
            dma((GROUPS,)),
            dma((len(BATCHES),)),
            dma((3,)),
            dma((owned,)),
            dma((len(BATCHES),)),
            dma((GROUPS + 1,)),
            pltpu.SemaphoreType.REGULAR((3,)),
        ],
        compiler_params=pltpu.CompilerParams(
            collective_id=0, has_side_effects=True, vmem_limit_bytes=58 << 20
        ),
    )(meson_nodes, term_nodes.T, weight_codes, resident_pick)


def body(meson_nodes, term_nodes, weight_codes, resident_pick):
    length, owned = lax.axis_size("node"), meson_nodes.shape[1]
    height = meson_nodes.shape[2]
    square = height == meson_nodes.shape[3]
    halves = lax.axis_size("sub") == 2 and lax.axis_size("rep") == 2
    fits = height % (8 * sum(UNITS)) == 0 and term_nodes.shape[0] <= (length - 2) * owned
    if square and halves and fits and owned == 2 and length == 4:
        return line_body(meson_nodes, term_nodes, weight_codes, resident_pick)
    return wide_body(meson_nodes, term_nodes, weight_codes, resident_pick)


def solution(mesh):
    in_specs = (P(None, ("grp", "node"), "sub", "rep"), P("grp", None), P("grp"), P("grp"))
    out_specs = P(None, ("grp", "node"), "sub", "rep")
    return jax.shard_map(body, mesh=mesh, in_specs=in_specs, out_specs=out_specs, check_vma=False)
```

```python
import functools

import jax
import jax.numpy as jnp
from jax import lax
from jax.experimental import pallas as pl
from jax.experimental.pallas import tpu as pltpu
from jax.sharding import PartitionSpec as P


def complex_step(full_left, segment):
    highest = lax.Precision.HIGHEST
    real_part = jnp.einsum(
        "kij,kjl->kil",
        full_left[0],
        segment[0],
        precision=highest,
        preferred_element_type=jnp.float32,
    ) - jnp.einsum(
        "kij,kjl->kil",
        full_left[1],
        segment[1],
        precision=highest,
        preferred_element_type=jnp.float32,
    )
    imag_part = jnp.einsum(
        "kij,kjl->kil",
        full_left[0],
        segment[1],
        precision=highest,
        preferred_element_type=jnp.float32,
    ) + jnp.einsum(
        "kij,kjl->kil",
        full_left[1],
        segment[0],
        precision=highest,
        preferred_element_type=jnp.float32,
    )
    return jnp.stack([real_part, imag_part])


def wide_body(meson_nodes, term_nodes, weight_codes, resident_pick):
    node_count = lax.axis_size("node")
    owned = meson_nodes.shape[1]
    row_count = meson_nodes.shape[2]
    col_count = meson_nodes.shape[3]
    band = row_count // node_count
    total_nodes = owned * node_count
    term_count = term_nodes.shape[0]
    banded = meson_nodes.reshape(2, owned, node_count, band * col_count)
    spread = lax.all_to_all(banded, "node", split_axis=2, concat_axis=1, tiled=True).reshape(
        2, total_nodes, band * col_count
    )
    leading = term_nodes[:, 0]
    trailing = term_nodes[:, 1]
    worker_ids = jnp.arange(node_count, dtype=jnp.int32)
    slot_count = term_count // node_count
    table = jnp.arange(slot_count, dtype=jnp.int32)[None, :] * node_count + worker_ids[:, None]
    active = jnp.ones(table.shape, jnp.float32)
    first_table = leading[table]
    second_table = trailing[table]
    factors = active * (weight_codes[table].astype(jnp.float32) - 3.5) * 0.5
    wanted = jnp.stack([first_table.T, second_table.T], axis=1)
    picked = jnp.take(spread, wanted, axis=1)
    fetched = lax.all_to_all(picked, "node", split_axis=3, concat_axis=3, tiled=True).reshape(
        2, slot_count, 2, row_count, col_count
    )
    left_rows = fetched[:, :, 0]
    right_band = fetched[:, :, 1]
    left_full = lax.all_gather(left_rows, "rep", axis=3, tiled=True)
    products = complex_step(left_full, lax.all_gather(right_band, "sub", axis=2, tiled=True))
    outgoing = products.reshape(2, slot_count, node_count, band * col_count)
    returned = lax.all_to_all(outgoing, "node", split_axis=2, concat_axis=1, tiled=True).reshape(
        2, node_count * slot_count, band * col_count
    )
    node_ids = jnp.arange(total_nodes, dtype=jnp.int32)
    incidence = (first_table.reshape(-1)[:, None] == node_ids[None, :]).astype(jnp.float32) + (
        second_table.reshape(-1)[:, None] == node_ids[None, :]
    ).astype(jnp.float32)
    mixing = factors.reshape(-1)[:, None] * incidence
    summed = jnp.einsum("mn,cmx->cnx", mixing, returned, precision=lax.Precision.HIGHEST)
    owner_sum = lax.all_to_all(
        summed.reshape(2, total_nodes, 1, band * col_count),
        "node",
        split_axis=1,
        concat_axis=2,
        tiled=True,
    ).reshape(2, owned, row_count, col_count)
    sum_full = lax.all_gather(owner_sum, "rep", axis=3, tiled=True)
    own_index = lax.axis_index("node")
    picks = lax.dynamic_slice_in_dim(resident_pick, own_index * owned, owned)
    resident = jnp.take(meson_nodes, picks, axis=1)
    return complex_step(sum_full, lax.all_gather(resident, "sub", axis=2, tiled=True))


MESH = pl.DeviceIdType.MESH
UNITS = (2,) * 14 + (1, 1, 1, 1)
LEADS = (4, 3, 3, 2, 2)
BATCHES = (2,) * 6 + (1,) * 6
GROUPS = 4
TAIL = (14, 15, 16, 17)


def split(value):
    high = value.astype(jnp.bfloat16)
    return high, (value - high.astype(jnp.float32)).astype(jnp.bfloat16)


def dot(p, q):
    return jnp.dot(p, q, preferred_element_type=jnp.float32)


def stacked_mul(l0, l1, right):
    rows = l0.shape[0]
    a, b = split(l0)
    c, d = split(l1)
    four = jnp.concatenate([a, b, c, d], axis=0)
    two = jnp.concatenate([a, c], axis=0)
    by_real, by_imag = dot(four, right(0)), dot(four, right(2))
    low_real, low_imag = dot(two, right(1)), dot(two, right(3))

    def part(value, i):
        return value[i * rows : (i + 1) * rows]

    def product(high, low, i):
        return part(high, 2 * i) + (part(high, 2 * i + 1) + part(low, i))

    real = product(by_real, low_real, 0) - product(by_imag, low_imag, 1)
    imag = product(by_imag, low_imag, 0) + product(by_real, low_real, 1)
    return real, imag


def plain_mul(l0, l1, right):
    def mul(value, i):
        high, low = split(value)
        return dot(high, right(i)) + (dot(high, right(i + 1)) + dot(low, right(i)))

    both, other, cross = mul(l0, 0), mul(l1, 2), mul(l0 + l1, 4)
    return both - other, cross - both - other


def sliced_mul(left, r0, r1):
    def mul(i, value):
        high, low = split(value)
        return dot(left(i), high) + (dot(left(i), low) + dot(left(i + 1), high))

    both, other, cross = mul(0, r0), mul(2, r1), mul(4, r0 + r1)
    return both - other, cross - both - other


def packed_mul(left, r0, r1):
    def mul(i, value):
        high, low = split(value)
        return dot(left(i), jnp.concatenate([high, high, low], axis=0))

    both, other, cross = mul(0, r0), mul(1, r1), mul(2, r0 + r1)
    return both - other, cross - both - other


def pieces_of(height):
    unit = height // sum(UNITS)
    pieces, at = [], 0
    for size in UNITS:
        pieces.append((at, size * unit))
        at += size * unit
    return pieces


def arrivals_of(pieces):
    order, sent = [], 0
    for r in range(len(pieces)):
        lead = LEADS[r] if r < len(LEADS) else 1
        while sent < min(r + lead, len(pieces)):
            order.append((0, sent))
            sent += 1
        order.append((1, r))
    return order


def plan_of(order, pieces, height):
    after = {
        (0, 1): [("pass", 1), ("right", 0), ("right", 1), ("right", 2), ("right", 3), ("left", 0)],
        (0, 2): [("pass", 3), ("left", 1)],
        (1, 0): [("pass", 5), ("facing", 0)],
        (0, 4): [("pass", 7)],
        (1, 3): [("pass", 9), ("facing", 1)],
        (1, 4): [("pass", 11)],
        (1, 5): [("facing", 2), ("end facing", 3), ("end turn", 0), ("end turn", 1)],
        (0, 6): [("pass", 13)],
        (1, 6): [("end turn", 2)],
        (1, 7): [("mid facing", 3), ("mid turn", 0)],
        (0, 8): [("pass", 17), ("mid turn", 1), ("mid turn", 2)],
        (1, 8): [("turn", 3), ("square", 0)],
        (0, 9): [("square", 1)],
        (1, 9): [("square", 2)],
        (0, 10): [("turn", 4), ("square", 3)],
        (1, 10): [("mine", 0)],
        (0, 11): [("up", 0)],
        (1, 11): [("up", 1)],
        (0, 12): [("turn", 5)],
        (1, 12): [("up", 2)],
        (0, 13): [("turn", 6)],
        (1, 13): [("theirs", 0)],
        (0, 14): [("turn", 7)],
        (1, 14): [("up", 3)],
        (0, 15): [("mine", 1)],
        (1, 15): [("turn", 8)],
        (1, 16): [("turn", 9)],
        (1, 17): [("turn", 10), ("turn", 11), ("late", 0), ("theirs", 1), ("mine", 2), ("up", 4), ("theirs", 2)],
    }
    plan = []
    for kind, r in order:
        plan.append(("far" if kind else "near", r))
        plan += after.get((kind, r), [])
    return plan


def line_kernel(
    length, owned, terms,
    x_ref, tn_any, wc_any, rp_any, out_ref,
    tn_ref, wc_ref, rp_ref, held, faced, outer, inner, far, near_pick, far_pick,
    mixes, turned, turned_far, lefts, packs, rights, squares,
    loc_sem, z_send, z_recv, o_recv, x_send, x_recv, t_recv, c_send, c_recv, m_recv, ready,
):
    z = lax.axis_index("node")
    x = lax.axis_index("sub")
    c = lax.axis_index("rep")
    g = lax.axis_index("grp")
    above = (g, z + 1, x, c)
    below = (g, z - 1, x, c)
    across = (g, z, 1 - x, c)
    twin = (g, z, x, 1 - c)
    own, facing = held.at[c], faced.at[c]
    height = x_ref.shape[2]
    pieces = pieces_of(height)
    count = len(pieces)
    order = arrivals_of(pieces)
    group = height // GROUPS
    groups = [(at, group) for at in range(0, height, group)]
    slices = [(0, 2 * group), (2 * group, group), (3 * group, group)]
    lifts = groups[:3] + [(3 * group, group // 2), (3 * group + group // 2, group // 2)]
    batches, first = [], 0
    for size in BATCHES:
        batches.append((pieces[first][0], sum(tall for _, tall in pieces[first : first + size])))
        first += size
    closing = {sum(BATCHES[: k + 1]) - 1: k for k in range(len(BATCHES))}
    raws = [(0, group // 2), (group // 2, group // 2)] + groups[1:]
    low = z < length // 2
    is_end = jnp.logical_or(z == 0, z == length - 1)
    is_mid = jnp.logical_not(is_end)
    end = jnp.where(low, 0, length - 1)
    far_end = length - 1 - end
    toward_end = (g, jnp.where(low, z - 1, z + 1), x, c)
    toward_mid = (g, jnp.where(low, z + 1, z - 1), x, c)

    def remote(src, dst, send, recv, device):
        return pltpu.make_async_remote_copy(
            src_ref=src, dst_ref=dst, send_sem=send, recv_sem=recv, device_id=device, device_id_type=MESH
        )

    def rows(r):
        return pl.ds(*pieces[r])

    def raw_copy(k):
        span = pl.ds(*raws[k])
        return remote(
            x_ref.at[:, :, span], outer.at[:, :, span], z_send.at[0], o_recv.at[k], toward_mid
        )

    def own_copy(r):
        return remote(
            x_ref.at[:, :, rows(r)], inner.at[:, :, rows(r)], z_send.at[1], z_recv.at[0, r], toward_mid
        )

    def pass_copy(r):
        return remote(
            outer.at[:, :, rows(r)], far.at[:, :, rows(r)], z_send.at[2], z_recv.at[1, r], toward_mid
        )

    def near_copy(r):
        return remote(
            near_pick.at[:, :, rows(r)], inner.at[:, :, rows(r)], z_send.at[3], z_recv.at[0, r], toward_end
        )

    def far_copy(r):
        return remote(
            far_pick.at[:, :, rows(r)], far.at[:, :, rows(r)], z_send.at[4], z_recv.at[1, r], toward_end
        )

    def x_copy(k):
        span = pl.ds(*groups[k])
        return remote(
            x_ref.at[:, :, span], facing.at[:, :, span], x_send.at[0], x_recv.at[k], across
        )

    def turned_copy(k):
        span = pl.ds(*batches[k])
        return remote(
            turned.at[:, :, span], turned_far.at[:, :, span], x_send.at[1], t_recv.at[slice_of(k)], across
        )

    def slice_of(k):
        return max(i for i, (at, _) in enumerate(slices) if at <= batches[k][0])

    def c_copy(slot):
        return remote(x_ref, held.at[slot], c_send.at[0], c_recv.at[0], twin)

    def face_copy(slot, span):
        part = faced.at[slot, :, :, span]
        return remote(part, part, c_send.at[2], c_recv.at[1], twin)

    tail_span = pl.ds(pieces[TAIL[0]][0], sum(pieces[r][1] for r in TAIL))

    def mix_copy(slot, k):
        span = pl.ds(*batches[k])
        tail = batches[k][0] >= pieces[TAIL[0]][0]
        part = mixes.at[slot, pl.ds(owned, owned), :, span] if tail else mixes.at[slot, :, :, span]
        return remote(part, part, c_send.at[1], m_recv.at[k], twin)

    def late_copy(slot):
        part = mixes.at[slot, pl.ds(0, owned), :, tail_span]
        return remote(part, part, c_send.at[1], m_recv.at[len(batches)], twin)

    tables = [
        pltpu.make_async_copy(src, dst, loc_sem.at[1 + i])
        for i, (src, dst) in enumerate(((tn_any, tn_ref), (wc_any, wc_ref), (rp_any, rp_ref)))
    ]
    barrier = pltpu.get_barrier_semaphore()
    ENTER = ((z < length - 1, above, z > 0, below), (x == 0, across, x == 1, across), (c == 1, twin, c == 0, twin))
    waits = 0
    for early, later_device, late, _ in ENTER:

        @pl.when(early)
        def _():
            pl.semaphore_signal(barrier, inc=1, device_id=later_device, device_id_type=MESH)

        waits = waits + late.astype(jnp.int32)

    @pl.when(waits > 0)
    def _():
        pl.semaphore_wait(barrier, waits)

    for i, (_, _, late, early_device) in enumerate(ENTER):

        @pl.when(late)
        def _():
            pl.semaphore_signal(ready.at[i], inc=1, device_id=early_device, device_id_type=MESH)

    def meet(i):
        @pl.when(ENTER[i][0])
        def _():
            pl.semaphore_wait(ready.at[i], 1)

    first_own = order[: order.index((1, 0))]
    passing = {"sent": len(first_own), "raw": 0}

    def send_until(r):
        last = order.index((1, r)) + 1

        @pl.when(is_mid)
        def _():
            for kind, p in order[passing["sent"] : last]:
                if kind == 0:
                    own_copy(p).start()
                else:
                    while passing["raw"] == 0 or sum(raws[passing["raw"] - 1]) < sum(pieces[p]):
                        raw_copy(passing["raw"]).wait_recv()
                        passing["raw"] += 1
                    pass_copy(p).start()

        passing["sent"] = last

    def open_sends():
        @pl.when(is_end)
        def _():
            for k in range(len(raws)):
                raw_copy(k).start()

        @pl.when(is_mid)
        def _():
            for _, p in first_own:
                own_copy(p).start()

    @pl.when(jnp.logical_not(low))
    def _():
        open_sends()

    meet(0)

    @pl.when(low)
    def _():
        open_sends()

    meet(2)
    c_copy(c).start()
    local = pltpu.make_async_copy(x_ref, own, loc_sem.at[0])
    local.start()
    for table in tables:
        table.start()
    meet(1)
    for k in range(GROUPS):
        x_copy(k).start()

    for table in tables:
        table.wait()
    firsts = [tn_ref[0, t] for t in range(terms)]
    seconds = [tn_ref[1, t] for t in range(terms)]
    factors = [(wc_ref[t].astype(jnp.float32) - 3.5) * 0.5 for t in range(terms)]
    choices = [rp_ref[z * owned + n] for n in range(owned)]
    spots = (length - 2) * owned

    def holds(owner, n):
        return jnp.logical_and(n >= owner * owned, n < owner * owned + owned)

    def rank_of(n):
        owner = n // owned
        return jnp.where(end == 0, owner, length - 1 - owner) * owned + n - owner * owned

    def node_of(rank):
        far_owner = rank // owned
        return jnp.where(end == 0, far_owner, length - 1 - far_owner) * owned + rank % owned

    def partner_ranks():
        ranks = []
        for a, b in zip(firsts, seconds):
            here, there = holds(end, a), holds(end, b)
            rank = jnp.where(here, rank_of(b), rank_of(a))
            ranks.append(jnp.where(here != there, rank, owned))
        below_rank, found = length * owned, []
        for _ in range(spots):
            best = owned
            for rank in ranks:
                best = jnp.where(jnp.logical_and(rank < below_rank, rank > best), rank, best)
            found.append(best)
            below_rank = best
        return found[::-1]

    wanted = partner_ranks()
    spot_nodes = []
    for i in range(spots):
        node = node_of(wanted[i])
        if i < spots - 1:
            node = jnp.where(wanted[i] == wanted[i + 1], -1, node)
        spot_nodes.append(node)
    home = z * owned
    near_mid = jnp.where(low, z + 1, z - 1) * owned
    entry_nodes = [home + j for j in range(owned)]
    entry_nodes += [jnp.where(is_mid, near_mid + j, spot_nodes[j]) for j in range(owned)]
    entry_nodes += [jnp.where(is_mid, far_end * owned + j, spot_nodes[owned + j]) for j in range(owned)]
    entry_nodes += [end * owned + j for j in range(owned)]
    zero = jnp.float32(0)

    def weight_of(keys, partners, n, node):
        total = zero
        for t in range(terms):
            match = jnp.logical_and(keys[t] == n, partners[t] == node)
            total = total + jnp.where(match, factors[t], zero)
        return total

    def weights_for(base):
        return [
            [weight_of(keys, partners, base + n, node) for node in entry_nodes]
            for keys, partners in ((seconds, firsts), (firsts, seconds))
            for n in range(owned)
        ]

    weights, end_weights = weights_for(home), weights_for(end * owned)

    def weighted(row, parts):
        total = row[0] * parts[0]
        for value, part in zip(row[1:], parts[1:]):
            total = total + value * part
        return total

    def blend(r, whole, tail=False):
        for m in range(2):
            parts = [ref[m, j, rows(r)] for ref in (own, inner, far) for j in range(owned)]
            if whole:
                parts += [outer[m, j, rows(r)] for j in range(owned)]
            for q, row in enumerate(weights):
                mixes[c, q, m, rows(r)] = weighted(row, parts)
            if tail:
                for q, row in enumerate(end_weights):
                    dst = far_pick if q < owned else near_pick
                    dst[m, q % owned, rows(r)] = weighted(row, parts)

    def pick(dst, i, spot, r, sources):
        for m in range(2):
            chosen = sources[0][0][m, sources[0][1], rows(r)]
            for k, (ref, j) in enumerate(sources[1:]):
                chosen = jnp.where(wanted[spot] == owned + 1 + k, ref[m, j, rows(r)], chosen)
            dst[m, i, rows(r)] = chosen

    ranked = [(ref, j) for ref in (own, inner, far) for j in range(owned)]

    def arrive(kind, r):
        if r in TAIL:
            return arrive_tail(kind, r)

        @pl.when(is_mid)
        def _():
            if kind == 0:
                own_copy(r).wait_recv()
                for i in range(owned):
                    pick(near_pick, i, i, r, ranked[: owned + 1 + i])
                near_copy(r).start()
            else:
                pass_copy(r).wait_recv()
                for i in range(owned):
                    pick(far_pick, i, owned + i, r, ranked[: 2 * owned + 1 + i])
                far_copy(r).start()
                blend(r, True)

        @pl.when(is_end)
        def _():
            if kind == 0:
                near_copy(r).wait_recv()
            else:
                far_copy(r).wait_recv()
                blend(r, False)

        if kind == 1 and r in closing:
            mix_copy(c, closing[r]).start()

    def arrive_tail(kind, r):
        @pl.when(is_mid)
        def _():
            if kind == 0:
                own_copy(r).wait_recv()
            else:
                pass_copy(r).wait_recv()
                blend(r, True, True)
                near_copy(r).start()
                if r > TAIL[0]:
                    far_copy(r - 1).start()
                if r == TAIL[-1]:
                    far_copy(r).start()

        if kind == 1:

            @pl.when(is_end)
            def _():
                near_copy(r).wait_recv()
                for n in range(owned):
                    for m in range(2):
                        mixes[c, owned + n, m, rows(r)] = inner[m, n, rows(r)]

            mix_copy(c, closing[r]).start()

    def late(_):
        @pl.when(is_end)
        def _():
            for r in TAIL:
                far_copy(r).wait_recv()
                for n in range(owned):
                    for m in range(2):
                        mixes[c, n, m, rows(r)] = far[m, n, rows(r)]

        late_copy(c).start()

    def clear():
        out_ref[...] = jnp.zeros_like(out_ref)

    def put_right(ref, h, k):
        span = pl.ds(*groups[k])
        for j in range(owned):
            re, im = ref[0, j, span], ref[1, j, span]
            for k, value in enumerate((re, im, re + im)):
                for i, part in enumerate(split(value)):
                    rights[j, 2 * k + i, h, span] = part

    def put_left(ref, h, n):
        re, im = ref[0, n], ref[1, n]
        for k, value in enumerate((re, im, re + im)):
            high, low_part = split(value)
            at, size = slices[0]
            lefts[n, 2 * k, h] = high[:, at : at + size]
            lefts[n, 2 * k + 1, h] = low_part[:, at : at + size]
            for i, (at, size) in enumerate(slices[1:]):
                part = high[:, at : at + size]
                packs[n, k, h, i] = jnp.concatenate([part, low_part[:, at : at + size], part], axis=1)

    def prepare_facing(k):
        x_copy(k).wait_recv()
        face_copy(c, pl.ds(*groups[k])).start()
        put_right(facing, 1 - x, k)

    def prepare_left(n):
        put_left(own, c, n)
        if n == 0:
            c_copy(1 - c).wait_recv()
        put_left(held.at[1 - c], 1 - c, n)

    def right_of(n):
        return lambda i: rights[n, i].reshape(2 * height, height)

    def wide(ref, q, m, span):
        return jnp.concatenate([ref[h, q, m, span] for h in range(2)], axis=1)

    def turn(k):
        mix_copy(1 - c, k).wait_recv()
        span = pl.ds(*batches[k])
        for n in range(owned):
            q = owned + n
            parts = stacked_mul(wide(mixes, q, 0, span), wide(mixes, q, 1, span), right_of(choices[n]))
            for m in range(2):
                turned[n, m, span] = parts[m]
        turned_copy(k).start()

    def square(i):
        n, away = i % owned, i // owned
        ref, h = (faced, 1 - x) if away else (held, x)
        if i == owned:
            face_copy(1 - c, pl.ds(0, height)).wait_recv()
        left = [jnp.concatenate([ref[h2, m, n] for h2 in range(2)], axis=1) for m in range(2)]
        parts = plain_mul(left[0], left[1], right_of(choices[n]))
        for m in range(2):
            for k, part in enumerate(split(parts[m])):
                squares[n, 2 * m + k, h] = part

    def raise_up(k):
        span = pl.ds(*lifts[k])
        if k == len(lifts) - 1:
            late_copy(1 - c).wait_recv()
        for n in range(owned):
            right = lambda i: squares[n, i].reshape(2 * height, height)
            parts = stacked_mul(wide(mixes, n, 0, span), wide(mixes, n, 1, span), right)
            for m in range(2):
                out_ref[m, n, span] = out_ref[m, n, span] + parts[m]

    def add_slice(ref, h, k):
        at, size = slices[k]
        for n in range(owned):
            r0, r1 = ref[n, 0, at : at + size], ref[n, 1, at : at + size]
            if k == 0:
                parts = sliced_mul(lambda i: lefts[n, i, h], r0, r1)
            else:
                parts = packed_mul(lambda i: packs[n, i, h, k - 1], r0, r1)
            for m in range(2):
                out_ref[m, n] = out_ref[m, n] + parts[m]

    def add_theirs(k):
        at, size = slices[k]
        span = pl.ds(at, size)
        remote(
            turned.at[:, :, span], turned_far.at[:, :, span], x_send.at[1], t_recv.at[k], across
        ).wait_recv()
        add_slice(turned_far, 1 - x, k)

    clear()
    local.wait()

    plan = plan_of(order, pieces, height)
    actions = {
        "pass": send_until,
        "near": lambda r: arrive(0, r),
        "far": lambda r: arrive(1, r),
        "late": late,
        "right": lambda k: put_right(own, x, k),
        "left": prepare_left,
        "facing": prepare_facing,
        "turn": turn,
        "up": raise_up,
        "square": square,
        "mine": lambda k: add_slice(turned, x, k),
        "theirs": add_theirs,
    }
    for name, i in plan:
        with jax.named_scope(f"{name}{i}".replace(" ", "_")):
            where, _, what = name.rpartition(" ")
            if where:
                pl.when(is_end if where == "end" else is_mid)(functools.partial(actions[what], i))
            else:
                actions[what](i)

    remote(x_ref, facing, x_send.at[0], x_recv.at[0], across).wait_send()
    remote(turned, turned_far, x_send.at[1], t_recv.at[0], across).wait_send()
    c_copy(c).wait_send()
    remote(mixes.at[c], mixes.at[c], c_send.at[1], m_recv.at[0], twin).wait_send()
    face_copy(c, pl.ds(0, height)).wait_send()

    @pl.when(is_end)
    def _():
        remote(x_ref, outer, z_send.at[0], o_recv.at[0], toward_mid).wait_send()

    @pl.when(is_mid)
    def _():
        remote(x_ref, inner, z_send.at[1], z_recv.at[0, 0], toward_mid).wait_send()
        remote(outer, far, z_send.at[2], z_recv.at[1, 0], toward_mid).wait_send()
        remote(near_pick, inner, z_send.at[3], z_recv.at[0, 0], toward_end).wait_send()
        remote(far_pick, far, z_send.at[4], z_recv.at[1, 0], toward_end).wait_send()


def line_body(meson_nodes, term_nodes, weight_codes, resident_pick):
    length = lax.axis_size("node")
    _, owned, height, width = meson_nodes.shape
    terms = term_nodes.shape[0]
    block = (height, width)
    vmem = pl.BlockSpec(memory_space=pltpu.VMEM)
    dma = pltpu.SemaphoreType.DMA
    count = len(UNITS)
    whole = pltpu.VMEM((2, owned) + block, jnp.float32)
    return pl.pallas_call(
        functools.partial(line_kernel, length, owned, terms),
        out_shape=pltpu.VMEM(meson_nodes.shape, jnp.float32),
        in_specs=[pl.BlockSpec(memory_space=pl.ANY)] * 4,
        out_specs=vmem,
        scratch_shapes=[
            pltpu.SMEM((2, terms), jnp.int32),
            pltpu.SMEM(weight_codes.shape, jnp.int32),
            pltpu.SMEM(resident_pick.shape, jnp.int32),
        ]
        + [pltpu.VMEM((2, 2, owned) + block, jnp.float32)] * 2
        + [whole] * 5
        + [
            pltpu.VMEM((2, 2 * owned, 2) + block, jnp.float32),
            pltpu.VMEM((owned, 2) + block, jnp.float32),
            pltpu.VMEM((owned, 2) + block, jnp.float32),
            pltpu.VMEM((owned, 6, 2, height, width // 2), jnp.bfloat16),
            pltpu.VMEM((owned, 3, 2, 2, height, 3 * width // GROUPS), jnp.bfloat16),
            pltpu.VMEM((owned, 6, 2) + block, jnp.bfloat16),
            pltpu.VMEM((owned, 4, 2) + block, jnp.bfloat16),
            dma((4,)),
            dma((5,)),
            dma((2, count)),
            dma((GROUPS + 1,)),
            dma((2,)),
            dma((GROUPS,)),
            dma((3,)),
            dma((3,)),
            dma((owned,)),
            dma((len(BATCHES) + 1,)),
            pltpu.SemaphoreType.REGULAR((3,)),
        ],
        compiler_params=pltpu.CompilerParams(
            collective_id=0, has_side_effects=True, vmem_limit_bytes=58 << 20
        ),
    )(meson_nodes, term_nodes.T, weight_codes, resident_pick)


def body(meson_nodes, term_nodes, weight_codes, resident_pick):
    length, owned = lax.axis_size("node"), meson_nodes.shape[1]
    height = meson_nodes.shape[2]
    square = height == meson_nodes.shape[3]
    halves = lax.axis_size("sub") == 2 and lax.axis_size("rep") == 2
    fits = height % (8 * sum(UNITS)) == 0 and term_nodes.shape[0] <= (length - 2) * owned
    if square and halves and fits and owned == 2 and length == 4:
        return line_body(meson_nodes, term_nodes, weight_codes, resident_pick)
    return wide_body(meson_nodes, term_nodes, weight_codes, resident_pick)


def solution(mesh):
    in_specs = (P(None, ("grp", "node"), "sub", "rep"), P("grp", None), P("grp"), P("grp"))
    out_specs = P(None, ("grp", "node"), "sub", "rep")
    return jax.shard_map(body, mesh=mesh, in_specs=in_specs, out_specs=out_specs, check_vma=False)
```

```python
import functools

import jax
import jax.numpy as jnp
from jax import lax
from jax.experimental import pallas as pl
from jax.experimental.pallas import tpu as pltpu
from jax.sharding import PartitionSpec as P


def complex_step(full_left, segment):
    highest = lax.Precision.HIGHEST
    real_part = jnp.einsum(
        "kij,kjl->kil",
        full_left[0],
        segment[0],
        precision=highest,
        preferred_element_type=jnp.float32,
    ) - jnp.einsum(
        "kij,kjl->kil",
        full_left[1],
        segment[1],
        precision=highest,
        preferred_element_type=jnp.float32,
    )
    imag_part = jnp.einsum(
        "kij,kjl->kil",
        full_left[0],
        segment[1],
        precision=highest,
        preferred_element_type=jnp.float32,
    ) + jnp.einsum(
        "kij,kjl->kil",
        full_left[1],
        segment[0],
        precision=highest,
        preferred_element_type=jnp.float32,
    )
    return jnp.stack([real_part, imag_part])


def wide_body(meson_nodes, term_nodes, weight_codes, resident_pick):
    node_count = lax.axis_size("node")
    owned = meson_nodes.shape[1]
    row_count = meson_nodes.shape[2]
    col_count = meson_nodes.shape[3]
    band = row_count // node_count
    total_nodes = owned * node_count
    term_count = term_nodes.shape[0]
    banded = meson_nodes.reshape(2, owned, node_count, band * col_count)
    spread = lax.all_to_all(banded, "node", split_axis=2, concat_axis=1, tiled=True).reshape(
        2, total_nodes, band * col_count
    )
    leading = term_nodes[:, 0]
    trailing = term_nodes[:, 1]
    worker_ids = jnp.arange(node_count, dtype=jnp.int32)
    slot_count = term_count // node_count
    table = jnp.arange(slot_count, dtype=jnp.int32)[None, :] * node_count + worker_ids[:, None]
    active = jnp.ones(table.shape, jnp.float32)
    first_table = leading[table]
    second_table = trailing[table]
    factors = active * (weight_codes[table].astype(jnp.float32) - 3.5) * 0.5
    wanted = jnp.stack([first_table.T, second_table.T], axis=1)
    picked = jnp.take(spread, wanted, axis=1)
    fetched = lax.all_to_all(picked, "node", split_axis=3, concat_axis=3, tiled=True).reshape(
        2, slot_count, 2, row_count, col_count
    )
    left_rows = fetched[:, :, 0]
    right_band = fetched[:, :, 1]
    left_full = lax.all_gather(left_rows, "rep", axis=3, tiled=True)
    products = complex_step(left_full, lax.all_gather(right_band, "sub", axis=2, tiled=True))
    outgoing = products.reshape(2, slot_count, node_count, band * col_count)
    returned = lax.all_to_all(outgoing, "node", split_axis=2, concat_axis=1, tiled=True).reshape(
        2, node_count * slot_count, band * col_count
    )
    node_ids = jnp.arange(total_nodes, dtype=jnp.int32)
    incidence = (first_table.reshape(-1)[:, None] == node_ids[None, :]).astype(jnp.float32) + (
        second_table.reshape(-1)[:, None] == node_ids[None, :]
    ).astype(jnp.float32)
    mixing = factors.reshape(-1)[:, None] * incidence
    summed = jnp.einsum("mn,cmx->cnx", mixing, returned, precision=lax.Precision.HIGHEST)
    owner_sum = lax.all_to_all(
        summed.reshape(2, total_nodes, 1, band * col_count),
        "node",
        split_axis=1,
        concat_axis=2,
        tiled=True,
    ).reshape(2, owned, row_count, col_count)
    sum_full = lax.all_gather(owner_sum, "rep", axis=3, tiled=True)
    own_index = lax.axis_index("node")
    picks = lax.dynamic_slice_in_dim(resident_pick, own_index * owned, owned)
    resident = jnp.take(meson_nodes, picks, axis=1)
    return complex_step(sum_full, lax.all_gather(resident, "sub", axis=2, tiled=True))


MESH = pl.DeviceIdType.MESH
UNITS = (2,) * 14 + (1, 1, 1, 1)
RAW = 6
BATCHES = (2,) * 3 + (1,) * 12
GROUPS = 4


def split(value):
    high = value.astype(jnp.bfloat16)
    return high, (value - high.astype(jnp.float32)).astype(jnp.bfloat16)


def dot(p, q):
    return jnp.dot(p, q, preferred_element_type=jnp.float32)


def stacked_mul(l0, l1, right):
    rows = l0.shape[0]
    a, b = split(l0)
    c, d = split(l1)
    four = jnp.concatenate([a, b, c, d], axis=0)
    two = jnp.concatenate([a, c], axis=0)
    by_real, by_imag = dot(four, right(0)), dot(four, right(2))
    low_real, low_imag = dot(two, right(1)), dot(two, right(3))

    def part(value, i):
        return value[i * rows : (i + 1) * rows]

    def product(high, low, i):
        return part(high, 2 * i) + (part(high, 2 * i + 1) + part(low, i))

    real = product(by_real, low_real, 0) - product(by_imag, low_imag, 1)
    imag = product(by_imag, low_imag, 0) + product(by_real, low_real, 1)
    return real, imag


def plain_mul(l0, l1, right):
    def mul(value, i):
        high, low = split(value)
        return dot(high, right(i)) + (dot(high, right(i + 1)) + dot(low, right(i)))

    both, other, cross = mul(l0, 0), mul(l1, 2), mul(l0 + l1, 4)
    return both - other, cross - both - other


def sliced_mul(left, r0, r1):
    def mul(i, value):
        high, low = split(value)
        return dot(left(i), high) + (dot(left(i), low) + dot(left(i + 1), high))

    both, other, cross = mul(0, r0), mul(2, r1), mul(4, r0 + r1)
    return both - other, cross - both - other


def packed_mul(left, r0, r1):
    def mul(i, value):
        high, low = split(value)
        return dot(left(i), jnp.concatenate([high, high, low], axis=0))

    both, other, cross = mul(0, r0), mul(1, r1), mul(2, r0 + r1)
    return both - other, cross - both - other


def pieces_of(height):
    unit = height // sum(UNITS)
    pieces, at = [], 0
    for size in UNITS:
        pieces.append((at, size * unit))
        at += size * unit
    return pieces


def plan_of(role, count):
    first = list(range(RAW))
    rest = list(range(RAW, count))
    order = [("near", p) for p in first] + [("far", p) for p in first]
    order += [("near", p) for p in rest] + [("far", p) for p in rest]
    if role == "mid":
        after = {
            ("near", 0): [("right", 0), ("right", 1)],
            ("near", 1): [("pass", 0), ("right", 2), ("right", 3)],
            ("near", 2): [("left", 0)],
            ("near", 3): [("pass", 1), ("left", 1)],
            ("near", 4): [("facing", 0)],
            ("near", 5): [("pass", 2)],
            ("far", 1): [("pass", 3)],
            ("far", 2): [("facing", 1)],
            ("far", 3): [("pass", 4)],
            ("far", 5): [("pass", 5)],
            ("near", 6): [("facing", 2)],
            ("near", 7): [("pass", 6)],
            ("near", 9): [("pass", 7)],
            ("near", 10): [("facing", 3), ("turn", 0)],
            ("near", 11): [("turn", 1), ("turn", 2)],
            ("near", 12): [("square", 0), ("square", 1)],
            ("near", 13): [("square", 2)],
            ("near", 15): [("square", 3)],
            ("near", 17): [("square", 4), ("square", 5)],
            ("far", 6): [("square", 6)],
            ("far", 7): [("turn", 3), ("square", 7)],
            ("far", 8): [("turn", 4), ("up", 0)],
            ("far", 9): [("turn", 5), ("up", 1)],
            ("far", 10): [("turn", 6)],
            ("far", 11): [("turn", 7), ("mine", 0)],
            ("far", 12): [("turn", 8)],
            ("far", 13): [("turn", 9)],
            ("far", 14): [("turn", 10)],
            ("far", 15): [("turn", 11)],
            ("far", 16): [("turn", 12)],
            ("far", 17): [
                ("turn", 13), ("turn", 14), ("theirs", 0), ("up", 2), ("mine", 1), ("up", 3), ("theirs", 1), ("mine", 2),
                ("up", 4), ("theirs", 2),
            ],
        }
    else:
        after = {
            ("near", 0): [("right", 0), ("right", 1), ("right", 2), ("right", 3)],
            ("near", 1): [("left", 0), ("left", 1)],
            ("near", 3): [("facing", 0)],
            ("far", 0): [("facing", 1)],
            ("far", 4): [("facing", 2)],
            ("near", 6): [("facing", 3), ("turn", 0), ("turn", 1)],
            ("near", 7): [("turn", 2)],
            ("near", 8): [("turn", 3)],
            ("near", 9): [("turn", 4), ("square", 0)],
            ("near", 10): [("turn", 5), ("square", 1)],
            ("near", 11): [("turn", 6), ("square", 2)],
            ("near", 12): [("turn", 7), ("square", 3)],
            ("near", 13): [("turn", 8)],
            ("near", 15): [("turn", 9)],
            ("near", 17): [("turn", 10), ("turn", 11), ("turn", 12)],
            ("far", 6): [("turn", 13), ("turn", 14), ("square", 4)],
            ("far", 7): [("square", 5), ("square", 6)],
            ("far", 8): [("square", 7), ("up", 0)],
            ("far", 9): [("up", 1)],
            ("far", 10): [("mine", 0)],
            ("far", 11): [("theirs", 0)],
            ("far", 12): [("mine", 1), ("mine", 2)],
            ("far", 13): [("up", 2)],
            ("far", 14): [("theirs", 1)],
            ("far", 17): [("theirs", 2), ("up", 3), ("up", 4)],
        }
    plan = []
    for step in order:
        plan.append(step)
        plan += after.get(step, [])
    return plan


def line_kernel(
    length, owned, terms,
    x_ref, tn_any, wc_any, rp_any, out_ref,
    tn_ref, wc_ref, rp_ref, held, faced, outer, inner, far, near_pick, far_pick, near_slot, far_slot,
    mixes, turned, turned_far, lefts, packs, rights, squares,
    loc_sem, z_send, z_recv, o_recv, x_send, x_recv, t_recv, c_send, c_recv, m_recv, ready,
):
    z = lax.axis_index("node")
    x = lax.axis_index("sub")
    c = lax.axis_index("rep")
    g = lax.axis_index("grp")
    above = (g, z + 1, x, c)
    below = (g, z - 1, x, c)
    across = (g, z, 1 - x, c)
    twin = (g, z, x, 1 - c)
    own, facing = held.at[c], faced.at[c]
    height = x_ref.shape[2]
    pieces = pieces_of(height)
    count = len(pieces)
    group = height // GROUPS
    groups = [(at, group) for at in range(0, height, group)]
    slices = [(0, 2 * group), (2 * group, group), (3 * group, group)]
    lifts = groups[:3] + [(3 * group, group // 2), (3 * group + group // 2, group // 2)]
    batches, first = [], 0
    for size in BATCHES:
        batches.append((pieces[first][0], sum(tall for _, tall in pieces[first : first + size])))
        first += size
    closing = {sum(BATCHES[: k + 1]) - 1: k for k in range(len(BATCHES))}
    lifting = {max(p for p, (at, _) in enumerate(pieces) if at < sum(lift)): k for k, lift in enumerate(lifts)}
    raws = [(at, group // 2) for at in range(0, height, group // 2)]
    low = z < length // 2
    is_end = jnp.logical_or(z == 0, z == length - 1)
    is_mid = jnp.logical_not(is_end)
    end = jnp.where(low, 0, length - 1)
    far_end = length - 1 - end
    toward_end = (g, jnp.where(low, z - 1, z + 1), x, c)
    toward_mid = (g, jnp.where(low, z + 1, z - 1), x, c)

    def remote(src, dst, send, recv, device):
        return pltpu.make_async_remote_copy(
            src_ref=src, dst_ref=dst, send_sem=send, recv_sem=recv, device_id=device, device_id_type=MESH
        )

    def rows(r):
        return pl.ds(*pieces[r])

    def raw_copy(k):
        span = pl.ds(*raws[k])
        return remote(
            x_ref.at[:, :, span], outer.at[:, :, span], z_send.at[0], o_recv.at[k], toward_mid
        )

    def own_copy(r):
        return remote(
            x_ref.at[:, :, rows(r)], inner.at[:, :, rows(r)], z_send.at[1], z_recv.at[0, r], toward_mid
        )

    def pass_copy(r):
        return remote(
            outer.at[:, :, rows(r)], far.at[:, :, rows(r)], z_send.at[2], z_recv.at[1, r], toward_mid
        )

    def near_slot_copy(r):
        return remote(
            near_slot.at[:, :, rows(r)], inner.at[:, :, rows(r)], z_send.at[1], z_recv.at[0, r], toward_mid
        )

    def far_slot_copy(r):
        return remote(
            far_slot.at[:, :, rows(r)], far.at[:, :, rows(r)], z_send.at[2], z_recv.at[1, r], toward_mid
        )

    def near_copy(r):
        return remote(
            near_pick.at[:, :, rows(r)], inner.at[:, :, rows(r)], z_send.at[3], z_recv.at[0, r], toward_end
        )

    def far_copy(r):
        return remote(
            far_pick.at[:, :, rows(r)], far.at[:, :, rows(r)], z_send.at[4], z_recv.at[1, r], toward_end
        )

    def x_copy(k):
        span = pl.ds(*groups[k])
        return remote(
            x_ref.at[:, :, span], facing.at[:, :, span], x_send.at[0], x_recv.at[k], across
        )

    def turned_copy(k):
        span = pl.ds(*batches[k])
        return remote(
            turned.at[:, :, span], turned_far.at[:, :, span], x_send.at[1], t_recv.at[slice_of(k)], across
        )

    def slice_of(k):
        return max(i for i, (at, _) in enumerate(slices) if at <= batches[k][0])

    def c_copy(slot):
        return remote(x_ref, held.at[slot], c_send.at[0], c_recv.at[0], twin)

    def face_copy(slot, span):
        part = faced.at[slot, :, :, span]
        return remote(part, part, c_send.at[2], c_recv.at[1], twin)

    def mix_copy(slot, k):
        part = mixes.at[slot, :, pl.ds(owned, owned), pl.ds(*batches[k])]
        return remote(part, part, c_send.at[1], m_recv.at[k], twin)

    def late_copy(slot, k):
        part = mixes.at[slot, :, pl.ds(0, owned), pl.ds(*lifts[k])]
        return remote(part, part, c_send.at[1], m_recv.at[len(batches) + k], twin)

    tables = [
        pltpu.make_async_copy(src, dst, loc_sem.at[1 + i])
        for i, (src, dst) in enumerate(((tn_any, tn_ref), (wc_any, wc_ref), (rp_any, rp_ref)))
    ]
    barrier = pltpu.get_barrier_semaphore()
    ENTER = ((z < length - 1, above, z > 0, below), (x == 0, across, x == 1, across), (c == 1, twin, c == 0, twin))
    waits = 0
    for early, later_device, late, _ in ENTER:

        @pl.when(early)
        def _():
            pl.semaphore_signal(barrier, inc=1, device_id=later_device, device_id_type=MESH)

        waits = waits + late.astype(jnp.int32)

    @pl.when(waits > 0)
    def _():
        pl.semaphore_wait(barrier, waits)

    for i, (_, _, late, early_device) in enumerate(ENTER):

        @pl.when(late)
        def _():
            pl.semaphore_signal(ready.at[i], inc=1, device_id=early_device, device_id_type=MESH)

    def meet(i):
        @pl.when(ENTER[i][0])
        def _():
            pl.semaphore_wait(ready.at[i], 1)

    def open_sends():
        @pl.when(is_end)
        def _():
            for k in range(len(raws)):
                raw_copy(k).start()

        @pl.when(is_mid)
        def _():
            own_copy(0).start()

    @pl.when(jnp.logical_not(low))
    def _():
        open_sends()

    @pl.when(low)
    def _():
        meet(0)
        open_sends()

    meet(2)

    @pl.when(is_mid)
    def _():
        for p in range(1, RAW):
            own_copy(p).start()

    @pl.when(jnp.logical_not(low))
    def _():
        meet(0)

    c_copy(c).start()
    local = pltpu.make_async_copy(x_ref, own, loc_sem.at[0])
    local.start()
    for table in tables:
        table.start()
    meet(1)
    for k in range(GROUPS):
        x_copy(k).start()

    for table in tables:
        table.wait()
    firsts = [tn_ref[0, t] for t in range(terms)]
    seconds = [tn_ref[1, t] for t in range(terms)]
    factors = [(wc_ref[t].astype(jnp.float32) - 3.5) * 0.5 for t in range(terms)]
    choices = [rp_ref[z * owned + n] for n in range(owned)]
    spots = (length - 2) * owned

    def holds(owner, n):
        return jnp.logical_and(n >= owner * owned, n < owner * owned + owned)

    def rank_of(n):
        owner = n // owned
        return jnp.where(end == 0, owner, length - 1 - owner) * owned + n - owner * owned

    def node_of(rank):
        far_owner = rank // owned
        return jnp.where(end == 0, far_owner, length - 1 - far_owner) * owned + rank % owned

    def partner_ranks():
        ranks = []
        for a, b in zip(firsts, seconds):
            here, there = holds(end, a), holds(end, b)
            rank = jnp.where(here, rank_of(b), rank_of(a))
            ranks.append(jnp.where(here != there, rank, owned))
        below_rank, found = length * owned, []
        for _ in range(spots):
            best = owned
            for rank in ranks:
                best = jnp.where(jnp.logical_and(rank < below_rank, rank > best), rank, best)
            found.append(best)
            below_rank = best
        return found[::-1]

    wanted = partner_ranks()
    spot_nodes = []
    for i in range(spots):
        node = node_of(wanted[i])
        if i < spots - 1:
            node = jnp.where(wanted[i] == wanted[i + 1], -1, node)
        spot_nodes.append(node)
    home = z * owned
    near_mid = jnp.where(low, z + 1, z - 1) * owned
    zero = jnp.float32(0)

    def slots_of(nodes, consumer):
        flags = []
        for node in nodes:
            flag = jnp.int32(0)
            for a, b in zip(firsts, seconds):
                flag = jnp.where(jnp.logical_and(holds(consumer, a), b == node), 1, flag)
            flags.append(flag)
        total = sum(flags[1:], flags[0])
        places = []
        for i, flag in enumerate(flags):
            before = sum(flags[:i], jnp.int32(0))
            places.append(jnp.where(flag == 1, before, total + i - before))
        return places

    def weights_for(base, nodes):
        def weight_of(keys, partners, n, node):
            total = zero
            for t in range(terms):
                match = jnp.logical_and(keys[t] == n, partners[t] == node)
                total = total + jnp.where(match, factors[t], zero)
            return total

        return [
            [weight_of(keys, partners, base + n, node) for node in nodes]
            for keys, partners in ((seconds, firsts), (firsts, seconds))
            for n in range(owned)
        ]

    def weighted(row, parts):
        total = row[0] * parts[0]
        for value, part in zip(row[1:], parts[1:]):
            total = total + value * part
        return total

    def blend(dst, r, table, refs):
        for m in range(2):
            parts = [ref[m, j, rows(r)] for ref in refs for j in range(owned)]
            for q, row in enumerate(table):
                dst[m, q, rows(r)] = weighted(row, parts)

    def pick(dst, i, spot, r, sources):
        for m in range(2):
            chosen = sources[0][0][m, sources[0][1], rows(r)]
            for k, (ref, j) in enumerate(sources[1:]):
                chosen = jnp.where(wanted[spot] == owned + 1 + k, ref[m, j, rows(r)], chosen)
            dst[m, i, rows(r)] = chosen

    ranked = [(ref, j) for ref in (own, inner, far) for j in range(owned)]

    mine = mixes.at[c]

    def close(r, left, right):
        if right and r in closing:
            mix_copy(c, closing[r]).start()
        if left and r in lifting:
            late_copy(c, lifting[r]).start()

    def mid_actions():
        raw_nodes = [base + j for base in (near_mid, far_end * owned) for j in range(owned)]
        known = [home + j for j in range(owned)], [end * owned + j for j in range(owned)]
        raw_table = weights_for(home, known[0] + raw_nodes + known[1])
        tables = {}

        def prepare_tables():
            places = slots_of(raw_nodes, end)
            nodes = []
            for i in range(2 * owned):
                node = jnp.int32(0)
                for place, name in zip(places, raw_nodes):
                    node = jnp.where(place == i, name, node)
                nodes.append(node)
            tables["own"] = weights_for(home, known[0] + nodes + known[1])
            tables["end"] = weights_for(end * owned, known[0] + nodes + known[1])
            tables["places"] = slots_of(known[0] + known[1], far_end)

        def near(r):
            own_copy(r).wait_recv()
            if r < RAW:
                for i in range(owned):
                    pick(near_pick, i, i, r, ranked[: owned + 1 + i])
            else:
                rights_only = [row[: 2 * owned] + row[3 * owned :] for row in tables["end"][owned:]]
                blend(near_pick, r, rights_only, (own, inner, outer))
            near_copy(r).start()

        def far_in(r):
            pass_copy(r).wait_recv()
            if r < RAW:
                for i in range(owned):
                    pick(far_pick, i, owned + i, r, ranked[: 2 * owned + 1 + i])
            else:
                blend(far_pick, r, tables["end"][:owned], (own, inner, far, outer))
            far_copy(r).start()
            blend(mine, r, raw_table if r < RAW else tables["own"], (own, inner, far, outer))
            close(r, True, True)

        def pass_on(k):
            raw_copy(k).wait_recv()
            inside = [p for p, (at, _) in enumerate(pieces) if raws[k][0] <= at < sum(raws[k])]
            for p in inside:
                if p < RAW:
                    pass_copy(p).start()
                    continue
                if "places" not in tables:
                    prepare_tables()
                for m in range(2):
                    parts = [ref[m, j, rows(p)] for ref in (own, outer) for j in range(owned)]
                    for i in range(2 * owned):
                        chosen = parts[0]
                        for place, part in zip(tables["places"][1:], parts[1:]):
                            chosen = jnp.where(place == i, part, chosen)
                        (near_slot if i < owned else far_slot)[m, i % owned, rows(p)] = chosen
                near_slot_copy(p).start()
            if k == len(raws) - 1:
                for p in range(RAW, count):
                    far_slot_copy(p).start()

        return {"near": near, "far": far_in, "pass": pass_on}

    def end_actions():
        table = weights_for(home, [home + j for j in range(owned)] + spot_nodes)

        def near(r):
            near_copy(r).wait_recv()
            if r >= RAW:
                mixes[c, :, owned:, rows(r)] = inner[:, :, rows(r)]
                close(r, False, True)

        def far_in(r):
            far_copy(r).wait_recv()
            if r < RAW:
                blend(mine, r, table, (own, inner, far))
            else:
                mixes[c, :, :owned, rows(r)] = far[:, :, rows(r)]
            close(r, True, r < RAW)

        return {"near": near, "far": far_in}

    def clear():
        out_ref[...] = jnp.zeros_like(out_ref)

    def put_right(ref, h, k):
        span = pl.ds(*groups[k])
        for j in range(owned):
            re, im = ref[0, j, span], ref[1, j, span]
            for k, value in enumerate((re, im, re + im)):
                for i, part in enumerate(split(value)):
                    rights[j, 2 * k + i, h, span] = part

    def put_left(ref, h, n):
        re, im = ref[0, n], ref[1, n]
        for k, value in enumerate((re, im, re + im)):
            high, low_part = split(value)
            at, size = slices[0]
            lefts[n, 2 * k, h] = high[:, at : at + size]
            lefts[n, 2 * k + 1, h] = low_part[:, at : at + size]
            for i, (at, size) in enumerate(slices[1:]):
                part = high[:, at : at + size]
                packs[n, k, h, i] = jnp.concatenate([part, low_part[:, at : at + size], part], axis=1)

    def prepare_facing(k):
        x_copy(k).wait_recv()
        face_copy(c, pl.ds(*groups[k])).start()
        put_right(facing, 1 - x, k)

    def prepare_left(n):
        put_left(own, c, n)
        if n == 0:
            c_copy(1 - c).wait_recv()
        put_left(held.at[1 - c], 1 - c, n)

    def right_of(n):
        return lambda i: rights[n, i].reshape(2 * height, height)

    def wide(ref, q, m, span):
        return jnp.concatenate([ref[h, m, q, span] for h in range(2)], axis=1)

    def turn(k):
        mix_copy(1 - c, k).wait_recv()
        span = pl.ds(*batches[k])
        for n in range(owned):
            q = owned + n
            parts = stacked_mul(wide(mixes, q, 0, span), wide(mixes, q, 1, span), right_of(choices[n]))
            for m in range(2):
                turned[n, m, span] = parts[m]
        turned_copy(k).start()

    def square(i):
        n, quarter = i % owned, i // owned
        away, at = quarter // 2, quarter % 2 * (height // 2)
        ref, h = (faced, 1 - x) if away else (held, x)
        if i == 2 * owned:
            face_copy(1 - c, pl.ds(0, height)).wait_recv()
        span = pl.ds(at, height // 2)
        left = [jnp.concatenate([ref[h2, m, n, span] for h2 in range(2)], axis=1) for m in range(2)]
        parts = plain_mul(left[0], left[1], right_of(choices[n]))
        for m in range(2):
            for k, part in enumerate(split(parts[m])):
                squares[n, 2 * m + k, h, span] = part

    def raise_up(k):
        span = pl.ds(*lifts[k])
        late_copy(1 - c, k).wait_recv()
        for n in range(owned):
            right = lambda i: squares[n, i].reshape(2 * height, height)
            parts = stacked_mul(wide(mixes, n, 0, span), wide(mixes, n, 1, span), right)
            for m in range(2):
                out_ref[m, n, span] = out_ref[m, n, span] + parts[m]

    def add_slice(ref, h, k):
        at, size = slices[k]
        for n in range(owned):
            r0, r1 = ref[n, 0, at : at + size], ref[n, 1, at : at + size]
            if k == 0:
                parts = sliced_mul(lambda i: lefts[n, i, h], r0, r1)
            else:
                parts = packed_mul(lambda i: packs[n, i, h, k - 1], r0, r1)
            for m in range(2):
                out_ref[m, n] = out_ref[m, n] + parts[m]

    def add_theirs(k):
        at, size = slices[k]
        span = pl.ds(at, size)
        remote(
            turned.at[:, :, span], turned_far.at[:, :, span], x_send.at[1], t_recv.at[k], across
        ).wait_recv()
        add_slice(turned_far, 1 - x, k)

    clear()
    local.wait()

    shared = {
        "right": lambda k: put_right(own, x, k),
        "left": prepare_left,
        "facing": prepare_facing,
        "turn": turn,
        "square": square,
        "up": raise_up,
        "mine": lambda k: add_slice(turned, x, k),
        "theirs": add_theirs,
    }

    def run(role, own_actions):
        actions = {**shared, **own_actions()}
        for name, i in plan_of(role, count):
            with jax.named_scope(f"{name}{i}"):
                actions[name](i)

    @pl.when(is_mid)
    def _():
        run("mid", mid_actions)

    @pl.when(is_end)
    def _():
        run("end", end_actions)

    remote(x_ref, facing, x_send.at[0], x_recv.at[0], across).wait_send()
    remote(turned, turned_far, x_send.at[1], t_recv.at[0], across).wait_send()
    c_copy(c).wait_send()
    remote(mixes.at[c], mixes.at[c], c_send.at[1], m_recv.at[0], twin).wait_send()
    face_copy(c, pl.ds(0, height)).wait_send()

    @pl.when(is_end)
    def _():
        remote(x_ref, outer, z_send.at[0], o_recv.at[0], toward_mid).wait_send()

    @pl.when(is_mid)
    def _():
        remote(x_ref, inner, z_send.at[1], z_recv.at[0, 0], toward_mid).wait_send()
        remote(outer, far, z_send.at[2], z_recv.at[1, 0], toward_mid).wait_send()
        remote(near_pick, inner, z_send.at[3], z_recv.at[0, 0], toward_end).wait_send()
        remote(far_pick, far, z_send.at[4], z_recv.at[1, 0], toward_end).wait_send()


def line_body(meson_nodes, term_nodes, weight_codes, resident_pick):
    length = lax.axis_size("node")
    _, owned, height, width = meson_nodes.shape
    terms = term_nodes.shape[0]
    block = (height, width)
    vmem = pl.BlockSpec(memory_space=pltpu.VMEM)
    dma = pltpu.SemaphoreType.DMA
    count = len(UNITS)
    whole = pltpu.VMEM((2, owned) + block, jnp.float32)
    return pl.pallas_call(
        functools.partial(line_kernel, length, owned, terms),
        out_shape=pltpu.VMEM(meson_nodes.shape, jnp.float32),
        in_specs=[pl.BlockSpec(memory_space=pl.ANY)] * 4,
        out_specs=vmem,
        scratch_shapes=[
            pltpu.SMEM((2, terms), jnp.int32),
            pltpu.SMEM(weight_codes.shape, jnp.int32),
            pltpu.SMEM(resident_pick.shape, jnp.int32),
        ]
        + [pltpu.VMEM((2, 2, owned) + block, jnp.float32)] * 2
        + [whole] * 7
        + [
            pltpu.VMEM((2, 2, 2 * owned) + block, jnp.float32),
            pltpu.VMEM((owned, 2) + block, jnp.float32),
            pltpu.VMEM((owned, 2) + block, jnp.float32),
            pltpu.VMEM((owned, 6, 2, height, width // 2), jnp.bfloat16),
            pltpu.VMEM((owned, 3, 2, 2, height, 3 * width // GROUPS), jnp.bfloat16),
            pltpu.VMEM((owned, 6, 2) + block, jnp.bfloat16),
            pltpu.VMEM((owned, 4, 2) + block, jnp.bfloat16),
            dma((4,)),
            dma((5,)),
            dma((2, count)),
            dma((2 * GROUPS,)),
            dma((2,)),
            dma((GROUPS,)),
            dma((3,)),
            dma((3,)),
            dma((owned,)),
            dma((len(BATCHES) + GROUPS + 1,)),
            pltpu.SemaphoreType.REGULAR((3,)),
        ],
        compiler_params=pltpu.CompilerParams(
            collective_id=0, has_side_effects=True, vmem_limit_bytes=58 << 20
        ),
    )(meson_nodes, term_nodes.T, weight_codes, resident_pick)


def body(meson_nodes, term_nodes, weight_codes, resident_pick):
    length, owned = lax.axis_size("node"), meson_nodes.shape[1]
    height = meson_nodes.shape[2]
    square = height == meson_nodes.shape[3]
    halves = lax.axis_size("sub") == 2 and lax.axis_size("rep") == 2
    fits = height % (8 * sum(UNITS)) == 0 and term_nodes.shape[0] <= (length - 2) * owned
    if square and halves and fits and owned == 2 and length == 4:
        return line_body(meson_nodes, term_nodes, weight_codes, resident_pick)
    return wide_body(meson_nodes, term_nodes, weight_codes, resident_pick)


def solution(mesh):
    in_specs = (P(None, ("grp", "node"), "sub", "rep"), P("grp", None), P("grp"), P("grp"))
    out_specs = P(None, ("grp", "node"), "sub", "rep")
    return jax.shard_map(body, mesh=mesh, in_specs=in_specs, out_specs=out_specs, check_vma=False)
```

```python
import functools

import jax
import jax.numpy as jnp
from jax import lax
from jax.experimental import pallas as pl
from jax.experimental.pallas import tpu as pltpu
from jax.sharding import PartitionSpec as P


def complex_step(full_left, segment):
    highest = lax.Precision.HIGHEST
    real_part = jnp.einsum(
        "kij,kjl->kil",
        full_left[0],
        segment[0],
        precision=highest,
        preferred_element_type=jnp.float32,
    ) - jnp.einsum(
        "kij,kjl->kil",
        full_left[1],
        segment[1],
        precision=highest,
        preferred_element_type=jnp.float32,
    )
    imag_part = jnp.einsum(
        "kij,kjl->kil",
        full_left[0],
        segment[1],
        precision=highest,
        preferred_element_type=jnp.float32,
    ) + jnp.einsum(
        "kij,kjl->kil",
        full_left[1],
        segment[0],
        precision=highest,
        preferred_element_type=jnp.float32,
    )
    return jnp.stack([real_part, imag_part])


def wide_body(meson_nodes, term_nodes, weight_codes, resident_pick):
    node_count = lax.axis_size("node")
    owned = meson_nodes.shape[1]
    row_count = meson_nodes.shape[2]
    col_count = meson_nodes.shape[3]
    band = row_count // node_count
    total_nodes = owned * node_count
    term_count = term_nodes.shape[0]
    banded = meson_nodes.reshape(2, owned, node_count, band * col_count)
    spread = lax.all_to_all(banded, "node", split_axis=2, concat_axis=1, tiled=True).reshape(
        2, total_nodes, band * col_count
    )
    leading = term_nodes[:, 0]
    trailing = term_nodes[:, 1]
    worker_ids = jnp.arange(node_count, dtype=jnp.int32)
    slot_count = term_count // node_count
    table = jnp.arange(slot_count, dtype=jnp.int32)[None, :] * node_count + worker_ids[:, None]
    active = jnp.ones(table.shape, jnp.float32)
    first_table = leading[table]
    second_table = trailing[table]
    factors = active * (weight_codes[table].astype(jnp.float32) - 3.5) * 0.5
    wanted = jnp.stack([first_table.T, second_table.T], axis=1)
    picked = jnp.take(spread, wanted, axis=1)
    fetched = lax.all_to_all(picked, "node", split_axis=3, concat_axis=3, tiled=True).reshape(
        2, slot_count, 2, row_count, col_count
    )
    left_rows = fetched[:, :, 0]
    right_band = fetched[:, :, 1]
    left_full = lax.all_gather(left_rows, "rep", axis=3, tiled=True)
    products = complex_step(left_full, lax.all_gather(right_band, "sub", axis=2, tiled=True))
    outgoing = products.reshape(2, slot_count, node_count, band * col_count)
    returned = lax.all_to_all(outgoing, "node", split_axis=2, concat_axis=1, tiled=True).reshape(
        2, node_count * slot_count, band * col_count
    )
    node_ids = jnp.arange(total_nodes, dtype=jnp.int32)
    incidence = (first_table.reshape(-1)[:, None] == node_ids[None, :]).astype(jnp.float32) + (
        second_table.reshape(-1)[:, None] == node_ids[None, :]
    ).astype(jnp.float32)
    mixing = factors.reshape(-1)[:, None] * incidence
    summed = jnp.einsum("mn,cmx->cnx", mixing, returned, precision=lax.Precision.HIGHEST)
    owner_sum = lax.all_to_all(
        summed.reshape(2, total_nodes, 1, band * col_count),
        "node",
        split_axis=1,
        concat_axis=2,
        tiled=True,
    ).reshape(2, owned, row_count, col_count)
    sum_full = lax.all_gather(owner_sum, "rep", axis=3, tiled=True)
    own_index = lax.axis_index("node")
    picks = lax.dynamic_slice_in_dim(resident_pick, own_index * owned, owned)
    resident = jnp.take(meson_nodes, picks, axis=1)
    return complex_step(sum_full, lax.all_gather(resident, "sub", axis=2, tiled=True))


MESH = pl.DeviceIdType.MESH
UNITS = (2,) * 14 + (1, 1, 1, 1)
RAW = 6
BATCHES = (2,) * 3 + (1,) * 8 + (2, 1, 1)
GROUPS = 4


def split(value):
    high = value.astype(jnp.bfloat16)
    return high, (value - high.astype(jnp.float32)).astype(jnp.bfloat16)


def dot(p, q):
    return jnp.dot(p, q, preferred_element_type=jnp.float32)


def stacked_mul(l0, l1, right):
    rows = l0.shape[0]
    a, b = split(l0)
    c, d = split(l1)
    four = jnp.concatenate([a, b, c, d], axis=0)
    two = jnp.concatenate([a, c], axis=0)
    by_real, by_imag = dot(four, right(0)), dot(four, right(2))
    low_real, low_imag = dot(two, right(1)), dot(two, right(3))

    def part(value, i):
        return value[i * rows : (i + 1) * rows]

    def product(high, low, i):
        return part(high, 2 * i) + (part(high, 2 * i + 1) + part(low, i))

    real = product(by_real, low_real, 0) - product(by_imag, low_imag, 1)
    imag = product(by_imag, low_imag, 0) + product(by_real, low_real, 1)
    return real, imag


def plain_mul(l0, l1, right):
    def mul(value, i):
        high, low = split(value)
        return dot(high, right(i)) + (dot(high, right(i + 1)) + dot(low, right(i)))

    both, other, cross = mul(l0, 0), mul(l1, 2), mul(l0 + l1, 4)
    return both - other, cross - both - other


def sliced_mul(left, r0, r1):
    def mul(i, value):
        high, low = split(value)
        return dot(left(i), high) + (dot(left(i), low) + dot(left(i + 1), high))

    both, other, cross = mul(0, r0), mul(2, r1), mul(4, r0 + r1)
    return both - other, cross - both - other


def packed_mul(left, r0, r1):
    def mul(i, value):
        high, low = split(value)
        return dot(left(i), jnp.concatenate([high, high, low], axis=0))

    both, other, cross = mul(0, r0), mul(1, r1), mul(2, r0 + r1)
    return both - other, cross - both - other


def pieces_of(height):
    unit = height // sum(UNITS)
    pieces, at = [], 0
    for size in UNITS:
        pieces.append((at, size * unit))
        at += size * unit
    return pieces


def plan_of(role, count):
    first = list(range(RAW))
    rest = list(range(RAW, count))
    order = [("near", p) for p in first] + [("far", p) for p in first]
    order += [("near", p) for p in rest] + [("far", p) for p in rest]
    if role == "mid":
        after = {
            ("near", 0): [("right", 0), ("right", 1)],
            ("near", 1): [("pass", 0), ("right", 2), ("right", 3)],
            ("near", 2): [("left", 0)],
            ("near", 3): [("pass", 1), ("left", 1)],
            ("near", 4): [("facing", 0)],
            ("near", 5): [("pass", 2)],
            ("far", 1): [("pass", 3)],
            ("far", 2): [("facing", 1)],
            ("far", 3): [("pass", 4)],
            ("far", 5): [("pass", 5)],
            ("near", 6): [("facing", 2)],
            ("near", 7): [("pass", 6)],
            ("near", 9): [("pass", 7)],
            ("near", 10): [("facing", 3), ("turn", 0)],
            ("near", 11): [("turn", 1), ("turn", 2)],
            ("near", 12): [("square", 0), ("square", 1)],
            ("near", 13): [("square", 2)],
            ("near", 15): [("square", 3)],
            ("near", 17): [("square", 4), ("square", 5)],
            ("far", 6): [("square", 6)],
            ("far", 7): [("turn", 3), ("square", 7)],
            ("far", 8): [("turn", 4), ("up", 0)],
            ("far", 9): [("turn", 5), ("up", 1)],
            ("far", 10): [("turn", 6)],
            ("far", 11): [("turn", 7), ("mine", 0)],
            ("far", 12): [("turn", 8)],
            ("far", 13): [("turn", 9)],
            ("far", 14): [("turn", 10)],
            ("far", 17): [
                ("turn", 11), ("turn", 12), ("turn", 13), ("theirs", 0), ("up", 2), ("mine", 1), ("up", 3), ("theirs", 1), ("mine", 2),
                ("up", 4), ("theirs", 2),
            ],
        }
    else:
        after = {
            ("near", 0): [("right", 0), ("right", 1), ("right", 2), ("right", 3)],
            ("near", 1): [("left", 0), ("left", 1)],
            ("near", 3): [("facing", 0)],
            ("far", 0): [("facing", 1)],
            ("far", 4): [("facing", 2)],
            ("near", 6): [("facing", 3), ("turn", 0), ("turn", 1)],
            ("near", 7): [("turn", 2)],
            ("near", 8): [("turn", 3)],
            ("near", 9): [("turn", 4), ("square", 0)],
            ("near", 10): [("turn", 5), ("square", 1)],
            ("near", 11): [("turn", 6), ("square", 2)],
            ("near", 12): [("turn", 7), ("square", 3)],
            ("near", 13): [("turn", 8)],
            ("near", 15): [("turn", 9)],
            ("near", 17): [("turn", 10), ("turn", 11)],
            ("far", 6): [("turn", 12), ("turn", 13), ("square", 4)],
            ("far", 7): [("square", 5), ("square", 6)],
            ("far", 8): [("square", 7), ("up", 0)],
            ("far", 9): [("up", 1)],
            ("far", 10): [("mine", 0)],
            ("far", 11): [("theirs", 0)],
            ("far", 12): [("mine", 1), ("mine", 2)],
            ("far", 13): [("up", 2)],
            ("far", 14): [("theirs", 1)],
            ("far", 17): [("theirs", 2), ("up", 3), ("up", 4)],
        }
    plan = []
    for step in order:
        plan.append(step)
        plan += after.get(step, [])
    return plan


def line_kernel(
    length, owned, terms,
    x_ref, tn_any, wc_any, rp_any, out_ref,
    tn_ref, wc_ref, rp_ref, held, faced, outer, inner, far, near_pick, far_pick, near_slot, far_slot,
    mixes, turned, turned_far, lefts, packs, rights, squares,
    loc_sem, z_send, z_recv, o_recv, x_send, x_recv, t_recv, c_send, c_recv, m_recv, ready,
):
    z = lax.axis_index("node")
    x = lax.axis_index("sub")
    c = lax.axis_index("rep")
    g = lax.axis_index("grp")
    above = (g, z + 1, x, c)
    below = (g, z - 1, x, c)
    across = (g, z, 1 - x, c)
    twin = (g, z, x, 1 - c)
    own, facing = held.at[c], faced.at[c]
    height = x_ref.shape[2]
    pieces = pieces_of(height)
    count = len(pieces)
    group = height // GROUPS
    groups = [(at, group) for at in range(0, height, group)]
    slices = [(0, 2 * group), (2 * group, group), (3 * group, group)]
    lifts = groups[:3] + [(3 * group, group // 2), (3 * group + group // 2, group // 2)]
    batches, first = [], 0
    for size in BATCHES:
        batches.append((pieces[first][0], sum(tall for _, tall in pieces[first : first + size])))
        first += size
    closing = {sum(BATCHES[: k + 1]) - 1: k for k in range(len(BATCHES))}
    last = pieces[-1]
    shares = lifts[:-1] + [(lifts[-1][0], lifts[-1][1] - last[1]), last]
    lifting = {max(p for p, (at, _) in enumerate(pieces) if at < sum(share)): k for k, share in enumerate(shares)}
    raws = [(at, group // 2) for at in range(0, height, group // 2)]
    low = z < length // 2
    is_end = jnp.logical_or(z == 0, z == length - 1)
    is_mid = jnp.logical_not(is_end)
    end = jnp.where(low, 0, length - 1)
    far_end = length - 1 - end
    toward_end = (g, jnp.where(low, z - 1, z + 1), x, c)
    toward_mid = (g, jnp.where(low, z + 1, z - 1), x, c)

    def remote(src, dst, send, recv, device):
        return pltpu.make_async_remote_copy(
            src_ref=src, dst_ref=dst, send_sem=send, recv_sem=recv, device_id=device, device_id_type=MESH
        )

    def rows(r):
        return pl.ds(*pieces[r])

    def raw_copy(k):
        span = pl.ds(*raws[k])
        return remote(
            x_ref.at[:, :, span], outer.at[:, :, span], z_send.at[0], o_recv.at[k], toward_mid
        )

    def own_copy(r):
        return remote(
            x_ref.at[:, :, rows(r)], inner.at[:, :, rows(r)], z_send.at[1], z_recv.at[0, r], toward_mid
        )

    def pass_copy(r):
        return remote(
            outer.at[:, :, rows(r)], far.at[:, :, rows(r)], z_send.at[2], z_recv.at[1, r], toward_mid
        )

    def near_slot_copy(r):
        return remote(
            near_slot.at[:, :, rows(r)], inner.at[:, :, rows(r)], z_send.at[1], z_recv.at[0, r], toward_mid
        )

    def far_slot_copy(r):
        return remote(
            far_slot.at[:, :, rows(r)], far.at[:, :, rows(r)], z_send.at[2], z_recv.at[1, r], toward_mid
        )

    def near_copy(r):
        return remote(
            near_pick.at[:, :, rows(r)], inner.at[:, :, rows(r)], z_send.at[3], z_recv.at[0, r], toward_end
        )

    def far_copy(r):
        return remote(
            far_pick.at[:, :, rows(r)], far.at[:, :, rows(r)], z_send.at[4], z_recv.at[1, r], toward_end
        )

    def x_copy(k):
        span = pl.ds(*groups[k])
        return remote(
            x_ref.at[:, :, span], facing.at[:, :, span], x_send.at[0], x_recv.at[k], across
        )

    def turned_copy(k):
        span = pl.ds(*batches[k])
        return remote(
            turned.at[:, :, span], turned_far.at[:, :, span], x_send.at[1], t_recv.at[slice_of(k)], across
        )

    def slice_of(k):
        return max(i for i, (at, _) in enumerate(slices) if at <= batches[k][0])

    def c_copy(slot):
        return remote(x_ref, held.at[slot], c_send.at[0], c_recv.at[0], twin)

    def face_copy(slot, span):
        part = faced.at[slot, :, :, span]
        return remote(part, part, c_send.at[2], c_recv.at[1], twin)

    def mix_copy(slot, k):
        part = mixes.at[slot, :, pl.ds(owned, owned), pl.ds(*batches[k])]
        return remote(part, part, c_send.at[1], m_recv.at[k], twin)

    def late_copy(slot, k):
        part = mixes.at[slot, :, pl.ds(0, owned), pl.ds(*shares[k])]
        return remote(part, part, c_send.at[1], m_recv.at[len(batches) + k], twin)

    tables = [
        pltpu.make_async_copy(src, dst, loc_sem.at[1 + i])
        for i, (src, dst) in enumerate(((tn_any, tn_ref), (wc_any, wc_ref), (rp_any, rp_ref)))
    ]
    barrier = pltpu.get_barrier_semaphore()
    ENTER = ((z < length - 1, above, z > 0, below), (x == 0, across, x == 1, across), (c == 1, twin, c == 0, twin))
    waits = 0
    for early, later_device, late, _ in ENTER:

        @pl.when(early)
        def _():
            pl.semaphore_signal(barrier, inc=1, device_id=later_device, device_id_type=MESH)

        waits = waits + late.astype(jnp.int32)

    @pl.when(waits > 0)
    def _():
        pl.semaphore_wait(barrier, waits)

    for i, (_, _, late, early_device) in enumerate(ENTER):

        @pl.when(late)
        def _():
            pl.semaphore_signal(ready.at[i], inc=1, device_id=early_device, device_id_type=MESH)

    def meet(i):
        @pl.when(ENTER[i][0])
        def _():
            pl.semaphore_wait(ready.at[i], 1)

    def open_sends():
        @pl.when(is_end)
        def _():
            for k in range(len(raws)):
                raw_copy(k).start()

        @pl.when(is_mid)
        def _():
            own_copy(0).start()

    @pl.when(jnp.logical_not(low))
    def _():
        open_sends()

    @pl.when(low)
    def _():
        meet(0)
        open_sends()

    meet(2)

    @pl.when(is_mid)
    def _():
        for p in range(1, RAW):
            own_copy(p).start()

    @pl.when(jnp.logical_not(low))
    def _():
        meet(0)

    c_copy(c).start()
    local = pltpu.make_async_copy(x_ref, own, loc_sem.at[0])
    local.start()
    for table in tables:
        table.start()
    meet(1)
    for k in range(GROUPS):
        x_copy(k).start()

    for table in tables:
        table.wait()
    firsts = [tn_ref[0, t] for t in range(terms)]
    seconds = [tn_ref[1, t] for t in range(terms)]
    factors = [(wc_ref[t].astype(jnp.float32) - 3.5) * 0.5 for t in range(terms)]
    choices = [rp_ref[z * owned + n] for n in range(owned)]
    spots = (length - 2) * owned

    def holds(owner, n):
        return jnp.logical_and(n >= owner * owned, n < owner * owned + owned)

    def rank_of(n):
        owner = n // owned
        return jnp.where(end == 0, owner, length - 1 - owner) * owned + n - owner * owned

    def node_of(rank):
        far_owner = rank // owned
        return jnp.where(end == 0, far_owner, length - 1 - far_owner) * owned + rank % owned

    def partner_ranks():
        ranks = []
        for a, b in zip(firsts, seconds):
            here, there = holds(end, a), holds(end, b)
            rank = jnp.where(here, rank_of(b), rank_of(a))
            ranks.append(jnp.where(here != there, rank, owned))
        below_rank, found = length * owned, []
        for _ in range(spots):
            best = owned
            for rank in ranks:
                best = jnp.where(jnp.logical_and(rank < below_rank, rank > best), rank, best)
            found.append(best)
            below_rank = best
        return found[::-1]

    wanted = partner_ranks()
    spot_nodes = []
    for i in range(spots):
        node = node_of(wanted[i])
        if i < spots - 1:
            node = jnp.where(wanted[i] == wanted[i + 1], -1, node)
        spot_nodes.append(node)
    home = z * owned
    near_mid = jnp.where(low, z + 1, z - 1) * owned
    zero = jnp.float32(0)

    def slots_of(nodes, consumer):
        flags = []
        for node in nodes:
            flag = jnp.int32(0)
            for a, b in zip(firsts, seconds):
                flag = jnp.where(jnp.logical_and(holds(consumer, a), b == node), 1, flag)
            flags.append(flag)
        total = sum(flags[1:], flags[0])
        places = []
        for i, flag in enumerate(flags):
            before = sum(flags[:i], jnp.int32(0))
            places.append(jnp.where(flag == 1, before, total + i - before))
        return places

    def weights_for(base, nodes):
        def weight_of(keys, partners, n, node):
            total = zero
            for t in range(terms):
                match = jnp.logical_and(keys[t] == n, partners[t] == node)
                total = total + jnp.where(match, factors[t], zero)
            return total

        return [
            [weight_of(keys, partners, base + n, node) for node in nodes]
            for keys, partners in ((seconds, firsts), (firsts, seconds))
            for n in range(owned)
        ]

    def weighted(row, parts):
        total = row[0] * parts[0]
        for value, part in zip(row[1:], parts[1:]):
            total = total + value * part
        return total

    def blend(dst, r, table, refs):
        for m in range(2):
            parts = [ref[m, j, rows(r)] for ref in refs for j in range(owned)]
            for q, row in enumerate(table):
                dst[m, q, rows(r)] = weighted(row, parts)

    def pick(dst, i, spot, r, sources):
        for m in range(2):
            chosen = sources[0][0][m, sources[0][1], rows(r)]
            for k, (ref, j) in enumerate(sources[1:]):
                chosen = jnp.where(wanted[spot] == owned + 1 + k, ref[m, j, rows(r)], chosen)
            dst[m, i, rows(r)] = chosen

    ranked = [(ref, j) for ref in (own, inner, far) for j in range(owned)]

    mine = mixes.at[c]

    def close(r, left, right):
        if right and r in closing:
            mix_copy(c, closing[r]).start()
        if left and r in lifting:
            late_copy(c, lifting[r]).start()

    def mid_actions():
        raw_nodes = [base + j for base in (near_mid, far_end * owned) for j in range(owned)]
        known = [home + j for j in range(owned)], [end * owned + j for j in range(owned)]
        raw_table = weights_for(home, known[0] + raw_nodes + known[1])
        tables = {}

        def prepare_tables():
            places = slots_of(raw_nodes, end)
            nodes = []
            for i in range(2 * owned):
                node = jnp.int32(0)
                for place, name in zip(places, raw_nodes):
                    node = jnp.where(place == i, name, node)
                nodes.append(node)
            tables["own"] = weights_for(home, known[0] + nodes + known[1])
            tables["end"] = weights_for(end * owned, known[0] + nodes + known[1])
            tables["places"] = slots_of(known[0] + known[1], far_end)

        def near(r):
            own_copy(r).wait_recv()
            if r < RAW:
                for i in range(owned):
                    pick(near_pick, i, i, r, ranked[: owned + 1 + i])
            else:
                rights_only = [row[: 2 * owned] + row[3 * owned :] for row in tables["end"][owned:]]
                blend(near_pick, r, rights_only, (own, inner, outer))
            near_copy(r).start()

        def far_in(r):
            pass_copy(r).wait_recv()
            if r < RAW:
                for i in range(owned):
                    pick(far_pick, i, owned + i, r, ranked[: 2 * owned + 1 + i])
            else:
                blend(far_pick, r, tables["end"][:owned], (own, inner, far, outer))
            far_copy(r).start()
            blend(mine, r, raw_table if r < RAW else tables["own"], (own, inner, far, outer))
            close(r, True, True)

        def pass_on(k):
            raw_copy(k).wait_recv()
            inside = [p for p, (at, _) in enumerate(pieces) if raws[k][0] <= at < sum(raws[k])]
            for p in inside:
                if p < RAW:
                    pass_copy(p).start()
                    continue
                if "places" not in tables:
                    prepare_tables()
                for m in range(2):
                    parts = [ref[m, j, rows(p)] for ref in (own, outer) for j in range(owned)]
                    for i in range(2 * owned):
                        chosen = parts[0]
                        for place, part in zip(tables["places"][1:], parts[1:]):
                            chosen = jnp.where(place == i, part, chosen)
                        (near_slot if i < owned else far_slot)[m, i % owned, rows(p)] = chosen
                near_slot_copy(p).start()
            if k == len(raws) - 1:
                for p in range(RAW, count):
                    far_slot_copy(p).start()

        return {"near": near, "far": far_in, "pass": pass_on}

    def end_actions():
        table = weights_for(home, [home + j for j in range(owned)] + spot_nodes)

        def near(r):
            near_copy(r).wait_recv()
            if r >= RAW:
                mixes[c, :, owned:, rows(r)] = inner[:, :, rows(r)]
                close(r, False, True)

        def far_in(r):
            far_copy(r).wait_recv()
            if r < RAW:
                blend(mine, r, table, (own, inner, far))
            else:
                mixes[c, :, :owned, rows(r)] = far[:, :, rows(r)]
            close(r, True, r < RAW)

        return {"near": near, "far": far_in}

    def clear():
        out_ref[...] = jnp.zeros_like(out_ref)

    def put_right(ref, h, k):
        span = pl.ds(*groups[k])
        for j in range(owned):
            re, im = ref[0, j, span], ref[1, j, span]
            for k, value in enumerate((re, im, re + im)):
                for i, part in enumerate(split(value)):
                    rights[j, 2 * k + i, h, span] = part

    def put_left(ref, h, n):
        re, im = ref[0, n], ref[1, n]
        for k, value in enumerate((re, im, re + im)):
            high, low_part = split(value)
            at, size = slices[0]
            lefts[n, 2 * k, h] = high[:, at : at + size]
            lefts[n, 2 * k + 1, h] = low_part[:, at : at + size]
            for i, (at, size) in enumerate(slices[1:]):
                part = high[:, at : at + size]
                packs[n, k, h, i] = jnp.concatenate([part, low_part[:, at : at + size], part], axis=1)

    def prepare_facing(k):
        x_copy(k).wait_recv()
        face_copy(c, pl.ds(*groups[k])).start()
        put_right(facing, 1 - x, k)

    def prepare_left(n):
        put_left(own, c, n)
        if n == 0:
            c_copy(1 - c).wait_recv()
        put_left(held.at[1 - c], 1 - c, n)

    def right_of(n):
        return lambda i: rights[n, i].reshape(2 * height, height)

    def wide(ref, q, m, span):
        return jnp.concatenate([ref[h, m, q, span] for h in range(2)], axis=1)

    def turn(k):
        mix_copy(1 - c, k).wait_recv()
        span = pl.ds(*batches[k])
        for n in range(owned):
            q = owned + n
            parts = stacked_mul(wide(mixes, q, 0, span), wide(mixes, q, 1, span), right_of(choices[n]))
            for m in range(2):
                turned[n, m, span] = parts[m]
        turned_copy(k).start()

    def square(i):
        n, quarter = i % owned, i // owned
        away, at = quarter // 2, quarter % 2 * (height // 2)
        ref, h = (faced, 1 - x) if away else (held, x)
        if i == 2 * owned:
            face_copy(1 - c, pl.ds(0, height)).wait_recv()
        span = pl.ds(at, height // 2)
        left = [jnp.concatenate([ref[h2, m, n, span] for h2 in range(2)], axis=1) for m in range(2)]
        parts = plain_mul(left[0], left[1], right_of(choices[n]))
        for m in range(2):
            for k, part in enumerate(split(parts[m])):
                squares[n, 2 * m + k, h, span] = part

    def raise_up(k):
        span = pl.ds(*lifts[k])
        late_copy(1 - c, k).wait_recv()
        if k == len(lifts) - 1:
            late_copy(1 - c, k + 1).wait_recv()
        for n in range(owned):
            right = lambda i: squares[n, i].reshape(2 * height, height)
            parts = stacked_mul(wide(mixes, n, 0, span), wide(mixes, n, 1, span), right)
            for m in range(2):
                out_ref[m, n, span] = out_ref[m, n, span] + parts[m]

    def add_slice(ref, h, k):
        at, size = slices[k]
        for n in range(owned):
            r0, r1 = ref[n, 0, at : at + size], ref[n, 1, at : at + size]
            if k == 0:
                parts = sliced_mul(lambda i: lefts[n, i, h], r0, r1)
            else:
                parts = packed_mul(lambda i: packs[n, i, h, k - 1], r0, r1)
            for m in range(2):
                out_ref[m, n] = out_ref[m, n] + parts[m]

    def add_theirs(k):
        at, size = slices[k]
        span = pl.ds(at, size)
        remote(
            turned.at[:, :, span], turned_far.at[:, :, span], x_send.at[1], t_recv.at[k], across
        ).wait_recv()
        add_slice(turned_far, 1 - x, k)

    clear()
    local.wait()

    shared = {
        "right": lambda k: put_right(own, x, k),
        "left": prepare_left,
        "facing": prepare_facing,
        "turn": turn,
        "square": square,
        "up": raise_up,
        "mine": lambda k: add_slice(turned, x, k),
        "theirs": add_theirs,
    }

    def run(role, own_actions):
        actions = {**shared, **own_actions()}
        for name, i in plan_of(role, count):
            with jax.named_scope(f"{name}{i}"):
                actions[name](i)

    @pl.when(is_mid)
    def _():
        run("mid", mid_actions)

    @pl.when(is_end)
    def _():
        run("end", end_actions)

    remote(x_ref, facing, x_send.at[0], x_recv.at[0], across).wait_send()
    remote(turned, turned_far, x_send.at[1], t_recv.at[0], across).wait_send()
    c_copy(c).wait_send()
    remote(mixes.at[c], mixes.at[c], c_send.at[1], m_recv.at[0], twin).wait_send()
    face_copy(c, pl.ds(0, height)).wait_send()

    @pl.when(is_end)
    def _():
        remote(x_ref, outer, z_send.at[0], o_recv.at[0], toward_mid).wait_send()

    @pl.when(is_mid)
    def _():
        remote(x_ref, inner, z_send.at[1], z_recv.at[0, 0], toward_mid).wait_send()
        remote(outer, far, z_send.at[2], z_recv.at[1, 0], toward_mid).wait_send()
        remote(near_pick, inner, z_send.at[3], z_recv.at[0, 0], toward_end).wait_send()
        remote(far_pick, far, z_send.at[4], z_recv.at[1, 0], toward_end).wait_send()


def line_body(meson_nodes, term_nodes, weight_codes, resident_pick):
    length = lax.axis_size("node")
    _, owned, height, width = meson_nodes.shape
    terms = term_nodes.shape[0]
    block = (height, width)
    vmem = pl.BlockSpec(memory_space=pltpu.VMEM)
    dma = pltpu.SemaphoreType.DMA
    count = len(UNITS)
    whole = pltpu.VMEM((2, owned) + block, jnp.float32)
    return pl.pallas_call(
        functools.partial(line_kernel, length, owned, terms),
        out_shape=pltpu.VMEM(meson_nodes.shape, jnp.float32),
        in_specs=[pl.BlockSpec(memory_space=pl.ANY)] * 4,
        out_specs=vmem,
        scratch_shapes=[
            pltpu.SMEM((2, terms), jnp.int32),
            pltpu.SMEM(weight_codes.shape, jnp.int32),
            pltpu.SMEM(resident_pick.shape, jnp.int32),
        ]
        + [pltpu.VMEM((2, 2, owned) + block, jnp.float32)] * 2
        + [whole] * 7
        + [
            pltpu.VMEM((2, 2, 2 * owned) + block, jnp.float32),
            pltpu.VMEM((owned, 2) + block, jnp.float32),
            pltpu.VMEM((owned, 2) + block, jnp.float32),
            pltpu.VMEM((owned, 6, 2, height, width // 2), jnp.bfloat16),
            pltpu.VMEM((owned, 3, 2, 2, height, 3 * width // GROUPS), jnp.bfloat16),
            pltpu.VMEM((owned, 6, 2) + block, jnp.bfloat16),
            pltpu.VMEM((owned, 4, 2) + block, jnp.bfloat16),
            dma((4,)),
            dma((5,)),
            dma((2, count)),
            dma((2 * GROUPS,)),
            dma((2,)),
            dma((GROUPS,)),
            dma((3,)),
            dma((3,)),
            dma((owned,)),
            dma((len(BATCHES) + GROUPS + 2,)),
            pltpu.SemaphoreType.REGULAR((3,)),
        ],
        compiler_params=pltpu.CompilerParams(
            collective_id=0, has_side_effects=True, vmem_limit_bytes=58 << 20
        ),
    )(meson_nodes, term_nodes.T, weight_codes, resident_pick)


def body(meson_nodes, term_nodes, weight_codes, resident_pick):
    length, owned = lax.axis_size("node"), meson_nodes.shape[1]
    height = meson_nodes.shape[2]
    square = height == meson_nodes.shape[3]
    halves = lax.axis_size("sub") == 2 and lax.axis_size("rep") == 2
    fits = height % (8 * sum(UNITS)) == 0 and term_nodes.shape[0] <= (length - 2) * owned
    if square and halves and fits and owned == 2 and length == 4:
        return line_body(meson_nodes, term_nodes, weight_codes, resident_pick)
    return wide_body(meson_nodes, term_nodes, weight_codes, resident_pick)


def solution(mesh):
    in_specs = (P(None, ("grp", "node"), "sub", "rep"), P("grp", None), P("grp"), P("grp"))
    out_specs = P(None, ("grp", "node"), "sub", "rep")
    return jax.shard_map(body, mesh=mesh, in_specs=in_specs, out_specs=out_specs, check_vma=False)
```

```python
import functools

import jax
import jax.numpy as jnp
from jax import lax
from jax.experimental import pallas as pl
from jax.experimental.pallas import tpu as pltpu
from jax.sharding import PartitionSpec as P


def complex_step(full_left, segment):
    highest = lax.Precision.HIGHEST
    real_part = jnp.einsum(
        "kij,kjl->kil",
        full_left[0],
        segment[0],
        precision=highest,
        preferred_element_type=jnp.float32,
    ) - jnp.einsum(
        "kij,kjl->kil",
        full_left[1],
        segment[1],
        precision=highest,
        preferred_element_type=jnp.float32,
    )
    imag_part = jnp.einsum(
        "kij,kjl->kil",
        full_left[0],
        segment[1],
        precision=highest,
        preferred_element_type=jnp.float32,
    ) + jnp.einsum(
        "kij,kjl->kil",
        full_left[1],
        segment[0],
        precision=highest,
        preferred_element_type=jnp.float32,
    )
    return jnp.stack([real_part, imag_part])


def wide_body(meson_nodes, term_nodes, weight_codes, resident_pick):
    node_count = lax.axis_size("node")
    owned = meson_nodes.shape[1]
    row_count = meson_nodes.shape[2]
    col_count = meson_nodes.shape[3]
    band = row_count // node_count
    total_nodes = owned * node_count
    term_count = term_nodes.shape[0]
    banded = meson_nodes.reshape(2, owned, node_count, band * col_count)
    spread = lax.all_to_all(banded, "node", split_axis=2, concat_axis=1, tiled=True).reshape(
        2, total_nodes, band * col_count
    )
    leading = term_nodes[:, 0]
    trailing = term_nodes[:, 1]
    worker_ids = jnp.arange(node_count, dtype=jnp.int32)
    slot_count = term_count // node_count
    table = jnp.arange(slot_count, dtype=jnp.int32)[None, :] * node_count + worker_ids[:, None]
    active = jnp.ones(table.shape, jnp.float32)
    first_table = leading[table]
    second_table = trailing[table]
    factors = active * (weight_codes[table].astype(jnp.float32) - 3.5) * 0.5
    wanted = jnp.stack([first_table.T, second_table.T], axis=1)
    picked = jnp.take(spread, wanted, axis=1)
    fetched = lax.all_to_all(picked, "node", split_axis=3, concat_axis=3, tiled=True).reshape(
        2, slot_count, 2, row_count, col_count
    )
    left_rows = fetched[:, :, 0]
    right_band = fetched[:, :, 1]
    left_full = lax.all_gather(left_rows, "rep", axis=3, tiled=True)
    products = complex_step(left_full, lax.all_gather(right_band, "sub", axis=2, tiled=True))
    outgoing = products.reshape(2, slot_count, node_count, band * col_count)
    returned = lax.all_to_all(outgoing, "node", split_axis=2, concat_axis=1, tiled=True).reshape(
        2, node_count * slot_count, band * col_count
    )
    node_ids = jnp.arange(total_nodes, dtype=jnp.int32)
    incidence = (first_table.reshape(-1)[:, None] == node_ids[None, :]).astype(jnp.float32) + (
        second_table.reshape(-1)[:, None] == node_ids[None, :]
    ).astype(jnp.float32)
    mixing = factors.reshape(-1)[:, None] * incidence
    summed = jnp.einsum("mn,cmx->cnx", mixing, returned, precision=lax.Precision.HIGHEST)
    owner_sum = lax.all_to_all(
        summed.reshape(2, total_nodes, 1, band * col_count),
        "node",
        split_axis=1,
        concat_axis=2,
        tiled=True,
    ).reshape(2, owned, row_count, col_count)
    sum_full = lax.all_gather(owner_sum, "rep", axis=3, tiled=True)
    own_index = lax.axis_index("node")
    picks = lax.dynamic_slice_in_dim(resident_pick, own_index * owned, owned)
    resident = jnp.take(meson_nodes, picks, axis=1)
    return complex_step(sum_full, lax.all_gather(resident, "sub", axis=2, tiled=True))


MESH = pl.DeviceIdType.MESH
UNITS = (2,) * 14 + (1, 1, 1, 1)
RAW = 6
BATCHES = (2,) * 3 + (1,) * 12
GROUPS = 4


def split(value):
    high = value.astype(jnp.bfloat16)
    return high, (value - high.astype(jnp.float32)).astype(jnp.bfloat16)


def dot(p, q):
    return jnp.dot(p, q, preferred_element_type=jnp.float32)


def stacked_mul(l0, l1, right):
    rows = l0.shape[0]
    a, b = split(l0)
    c, d = split(l1)
    four = jnp.concatenate([a, b, c, d], axis=0)
    two = jnp.concatenate([a, c], axis=0)
    by_real, by_imag = dot(four, right(0)), dot(four, right(2))
    low_real, low_imag = dot(two, right(1)), dot(two, right(3))

    def part(value, i):
        return value[i * rows : (i + 1) * rows]

    def product(high, low, i):
        return part(high, 2 * i) + (part(high, 2 * i + 1) + part(low, i))

    real = product(by_real, low_real, 0) - product(by_imag, low_imag, 1)
    imag = product(by_imag, low_imag, 0) + product(by_real, low_real, 1)
    return real, imag


def plain_mul(l0, l1, right):
    def mul(value, i):
        high, low = split(value)
        return dot(high, right(i)) + (dot(high, right(i + 1)) + dot(low, right(i)))

    both, other, cross = mul(l0, 0), mul(l1, 2), mul(l0 + l1, 4)
    return both - other, cross - both - other


def sliced_mul(left, r0, r1):
    def mul(i, value):
        high, low = split(value)
        return dot(left(i), high) + (dot(left(i), low) + dot(left(i + 1), high))

    both, other, cross = mul(0, r0), mul(2, r1), mul(4, r0 + r1)
    return both - other, cross - both - other


def packed_mul(left, r0, r1):
    def mul(i, value):
        high, low = split(value)
        return dot(left(i), jnp.concatenate([high, high, low], axis=0))

    both, other, cross = mul(0, r0), mul(1, r1), mul(2, r0 + r1)
    return both - other, cross - both - other


def pieces_of(height):
    unit = height // sum(UNITS)
    pieces, at = [], 0
    for size in UNITS:
        pieces.append((at, size * unit))
        at += size * unit
    return pieces


def plan_of(role, count):
    first = list(range(RAW))
    rest = list(range(RAW, count))
    order = [("near", p) for p in first] + [("far", p) for p in first]
    order += [("near", p) for p in rest] + [("far", p) for p in rest]
    if role == "mid":
        after = {
            ("near", 0): [("right", 0), ("right", 1)],
            ("near", 1): [("pass", 0), ("right", 2), ("right", 3)],
            ("near", 2): [("left", 0)],
            ("near", 3): [("pass", 1), ("left", 1)],
            ("near", 4): [("facing", 0)],
            ("near", 5): [("pass", 2)],
            ("far", 1): [("pass", 3)],
            ("far", 2): [("facing", 1)],
            ("far", 3): [("pass", 4)],
            ("far", 5): [("pass", 5)],
            ("near", 6): [("facing", 2)],
            ("near", 7): [("pass", 6)],
            ("near", 9): [("pass", 7)],
            ("near", 10): [("facing", 3), ("turn", 0)],
            ("near", 11): [("turn", 1), ("turn", 2)],
            ("near", 12): [("square", 0), ("square", 1)],
            ("near", 13): [("square", 2)],
            ("near", 15): [("square", 3)],
            ("near", 17): [("square", 4), ("square", 5)],
            ("far", 6): [("square", 6)],
            ("far", 7): [("turn", 3), ("square", 7)],
            ("far", 8): [("turn", 4), ("up", 0)],
            ("far", 9): [("turn", 5), ("up", 1)],
            ("far", 10): [("turn", 6)],
            ("far", 11): [("turn", 7), ("mine", 0)],
            ("far", 12): [("turn", 8)],
            ("far", 13): [("turn", 9)],
            ("far", 14): [("turn", 10)],
            ("far", 15): [("turn", 11)],
            ("far", 16): [("turn", 12)],
            ("far", 17): [
                ("turn", 13), ("turn", 14), ("theirs", 0), ("up", 2), ("mine", 1), ("up", 3), ("theirs", 1), ("mine", 2),
                ("up", 4), ("theirs", 2),
            ],
        }
    else:
        after = {
            ("near", 0): [("right", 0), ("right", 1), ("right", 2), ("right", 3)],
            ("near", 1): [("left", 0), ("left", 1)],
            ("near", 3): [("facing", 0)],
            ("far", 0): [("facing", 1)],
            ("far", 4): [("facing", 2)],
            ("near", 6): [("facing", 3), ("turn", 0), ("turn", 1)],
            ("near", 7): [("turn", 2)],
            ("near", 8): [("turn", 3)],
            ("near", 9): [("turn", 4), ("square", 0)],
            ("near", 10): [("turn", 5), ("square", 1)],
            ("near", 11): [("turn", 6), ("square", 2)],
            ("near", 12): [("turn", 7), ("square", 3)],
            ("near", 13): [("turn", 8)],
            ("near", 15): [("turn", 9)],
            ("near", 17): [("turn", 10), ("turn", 11), ("turn", 12)],
            ("far", 6): [("turn", 13), ("turn", 14), ("square", 4)],
            ("far", 7): [("square", 5), ("square", 6)],
            ("far", 8): [("square", 7), ("up", 0)],
            ("far", 9): [("up", 1)],
            ("far", 10): [("mine", 0)],
            ("far", 11): [("theirs", 0)],
            ("far", 12): [("mine", 1), ("mine", 2)],
            ("far", 13): [("up", 2)],
            ("far", 14): [("theirs", 1)],
            ("far", 17): [("theirs", 2), ("up", 3), ("up", 4)],
        }
    plan = []
    for step in order:
        plan.append(step)
        plan += after.get(step, [])
    return plan


def line_kernel(
    length, owned, terms,
    x_ref, tn_any, wc_any, rp_any, out_ref,
    tn_ref, wc_ref, rp_ref, held, faced, outer, inner, far, near_pick, far_pick, near_slot, far_slot,
    mixes, turned, turned_far, lefts, packs, rights, squares,
    loc_sem, z_send, z_recv, o_recv, x_send, x_recv, t_recv, c_send, c_recv, m_recv, ready,
):
    z = lax.axis_index("node")
    x = lax.axis_index("sub")
    c = lax.axis_index("rep")
    g = lax.axis_index("grp")
    above = (g, z + 1, x, c)
    below = (g, z - 1, x, c)
    across = (g, z, 1 - x, c)
    twin = (g, z, x, 1 - c)
    own, facing = held.at[c], faced.at[c]
    height = x_ref.shape[2]
    pieces = pieces_of(height)
    count = len(pieces)
    group = height // GROUPS
    groups = [(at, group) for at in range(0, height, group)]
    slices = [(0, 2 * group), (2 * group, group), (3 * group, group)]
    lifts = groups[:3] + [(3 * group, group // 2), (3 * group + group // 2, group // 2)]
    batches, first = [], 0
    for size in BATCHES:
        batches.append((pieces[first][0], sum(tall for _, tall in pieces[first : first + size])))
        first += size
    closing = {sum(BATCHES[: k + 1]) - 1: k for k in range(len(BATCHES))}
    last = pieces[-1]
    shares = lifts[:-1] + [(lifts[-1][0], lifts[-1][1] - last[1]), last]
    lifting = {max(p for p, (at, _) in enumerate(pieces) if at < sum(share)): k for k, share in enumerate(shares)}
    raws = [(at, group // 2) for at in range(0, height, group // 2)]
    low = z < length // 2
    is_end = jnp.logical_or(z == 0, z == length - 1)
    is_mid = jnp.logical_not(is_end)
    end = jnp.where(low, 0, length - 1)
    far_end = length - 1 - end
    toward_end = (g, jnp.where(low, z - 1, z + 1), x, c)
    toward_mid = (g, jnp.where(low, z + 1, z - 1), x, c)

    def remote(src, dst, send, recv, device):
        return pltpu.make_async_remote_copy(
            src_ref=src, dst_ref=dst, send_sem=send, recv_sem=recv, device_id=device, device_id_type=MESH
        )

    def rows(r):
        return pl.ds(*pieces[r])

    def raw_copy(k):
        span = pl.ds(*raws[k])
        return remote(
            x_ref.at[:, :, span], outer.at[:, :, span], z_send.at[0], o_recv.at[k], toward_mid
        )

    def own_copy(r):
        return remote(
            x_ref.at[:, :, rows(r)], inner.at[:, :, rows(r)], z_send.at[0], z_recv.at[0, r], toward_mid
        )

    def pass_copy(r):
        return remote(
            outer.at[:, :, rows(r)], far.at[:, :, rows(r)], z_send.at[1], z_recv.at[1, r], toward_mid
        )

    def near_slot_copy(r):
        return remote(
            near_slot.at[:, :, rows(r)], inner.at[:, :, rows(r)], z_send.at[0], z_recv.at[0, r], toward_mid
        )

    def far_slot_copy(r):
        return remote(
            far_slot.at[:, :, rows(r)], far.at[:, :, rows(r)], z_send.at[1], z_recv.at[1, r], toward_mid
        )

    def near_copy(r):
        return remote(
            near_pick.at[:, :, rows(r)], inner.at[:, :, rows(r)], z_send.at[2], z_recv.at[0, r], toward_end
        )

    def far_copy(r):
        return remote(
            far_pick.at[:, :, rows(r)], far.at[:, :, rows(r)], z_send.at[3], z_recv.at[1, r], toward_end
        )

    def x_copy(k):
        span = pl.ds(*groups[k])
        return remote(
            x_ref.at[:, :, span], facing.at[:, :, span], x_send.at[0], x_recv.at[k], across
        )

    def turned_copy(k):
        span = pl.ds(*batches[k])
        return remote(
            turned.at[:, :, span], turned_far.at[:, :, span], x_send.at[1], t_recv.at[slice_of(k)], across
        )

    def slice_of(k):
        return max(i for i, (at, _) in enumerate(slices) if at <= batches[k][0])

    def c_copy(slot):
        return remote(x_ref, held.at[slot], c_send.at[0], c_recv.at[0], twin)

    def face_copy(slot, span):
        part = faced.at[slot, :, :, span]
        return remote(part, part, c_send.at[2], c_recv.at[1], twin)

    def mix_copy(slot, k):
        part = mixes.at[slot, :, pl.ds(owned, owned), pl.ds(*batches[k])]
        return remote(part, part, c_send.at[1], m_recv.at[k], twin)

    def late_copy(slot, k):
        part = mixes.at[slot, :, pl.ds(0, owned), pl.ds(*shares[k])]
        return remote(part, part, c_send.at[1], m_recv.at[len(batches) + k], twin)

    tables = [
        pltpu.make_async_copy(src, dst, loc_sem.at[1 + i])
        for i, (src, dst) in enumerate(((tn_any, tn_ref), (wc_any, wc_ref), (rp_any, rp_ref)))
    ]
    barrier = pltpu.get_barrier_semaphore()
    ENTER = ((z < length - 1, above, z > 0, below), (x == 0, across, x == 1, across), (c == 1, twin, c == 0, twin))
    waits = 0
    for early, later_device, late, _ in ENTER:

        @pl.when(early)
        def _():
            pl.semaphore_signal(barrier, inc=1, device_id=later_device, device_id_type=MESH)

        waits = waits + late.astype(jnp.int32)

    @pl.when(waits > 0)
    def _():
        pl.semaphore_wait(barrier, waits)

    for i, (_, _, late, early_device) in enumerate(ENTER):

        @pl.when(late)
        def _():
            pl.semaphore_signal(ready.at[i], inc=1, device_id=early_device, device_id_type=MESH)

    def meet(i):
        @pl.when(ENTER[i][0])
        def _():
            pl.semaphore_wait(ready.at[i], 1)

    def open_sends():
        @pl.when(is_end)
        def _():
            for k in range(len(raws)):
                raw_copy(k).start()

        @pl.when(is_mid)
        def _():
            own_copy(0).start()

    @pl.when(jnp.logical_not(low))
    def _():
        open_sends()

    @pl.when(low)
    def _():
        meet(0)
        open_sends()

    meet(2)

    @pl.when(is_mid)
    def _():
        for p in range(1, RAW):
            own_copy(p).start()

    @pl.when(jnp.logical_not(low))
    def _():
        meet(0)

    c_copy(c).start()
    local = pltpu.make_async_copy(x_ref, own, loc_sem.at[0])
    local.start()
    for table in tables:
        table.start()
    meet(1)
    for k in range(GROUPS):
        x_copy(k).start()

    for table in tables:
        table.wait()
    firsts = [tn_ref[0, t] for t in range(terms)]
    seconds = [tn_ref[1, t] for t in range(terms)]
    factors = [(wc_ref[t].astype(jnp.float32) - 3.5) * 0.5 for t in range(terms)]
    choices = [rp_ref[z * owned + n] for n in range(owned)]
    spots = (length - 2) * owned

    def holds(owner, n):
        return jnp.logical_and(n >= owner * owned, n < owner * owned + owned)

    def rank_of(n):
        owner = n // owned
        return jnp.where(end == 0, owner, length - 1 - owner) * owned + n - owner * owned

    def node_of(rank):
        far_owner = rank // owned
        return jnp.where(end == 0, far_owner, length - 1 - far_owner) * owned + rank % owned

    def partner_ranks():
        ranks = []
        for a, b in zip(firsts, seconds):
            here, there = holds(end, a), holds(end, b)
            rank = jnp.where(here, rank_of(b), rank_of(a))
            ranks.append(jnp.where(here != there, rank, owned))
        below_rank, found = length * owned, []
        for _ in range(spots):
            best = owned
            for rank in ranks:
                best = jnp.where(jnp.logical_and(rank < below_rank, rank > best), rank, best)
            found.append(best)
            below_rank = best
        return found[::-1]

    wanted = partner_ranks()
    spot_nodes = []
    for i in range(spots):
        node = node_of(wanted[i])
        if i < spots - 1:
            node = jnp.where(wanted[i] == wanted[i + 1], -1, node)
        spot_nodes.append(node)
    home = z * owned
    near_mid = jnp.where(low, z + 1, z - 1) * owned
    zero = jnp.float32(0)

    def slots_of(nodes, consumer):
        flags = []
        for node in nodes:
            flag = jnp.int32(0)
            for a, b in zip(firsts, seconds):
                flag = jnp.where(jnp.logical_and(holds(consumer, a), b == node), 1, flag)
            flags.append(flag)
        total = sum(flags[1:], flags[0])
        places = []
        for i, flag in enumerate(flags):
            before = sum(flags[:i], jnp.int32(0))
            places.append(jnp.where(flag == 1, before, total + i - before))
        return places

    def weights_for(base, nodes):
        def weight_of(keys, partners, n, node):
            total = zero
            for t in range(terms):
                match = jnp.logical_and(keys[t] == n, partners[t] == node)
                total = total + jnp.where(match, factors[t], zero)
            return total

        return [
            [weight_of(keys, partners, base + n, node) for node in nodes]
            for keys, partners in ((seconds, firsts), (firsts, seconds))
            for n in range(owned)
        ]

    def weighted(row, parts):
        total = row[0] * parts[0]
        for value, part in zip(row[1:], parts[1:]):
            total = total + value * part
        return total

    def blend(dst, r, table, refs):
        for m in range(2):
            parts = [ref[m, j, rows(r)] for ref in refs for j in range(owned)]
            for q, row in enumerate(table):
                dst[m, q, rows(r)] = weighted(row, parts)

    def pick(dst, i, spot, r, sources):
        for m in range(2):
            chosen = sources[0][0][m, sources[0][1], rows(r)]
            for k, (ref, j) in enumerate(sources[1:]):
                chosen = jnp.where(wanted[spot] == owned + 1 + k, ref[m, j, rows(r)], chosen)
            dst[m, i, rows(r)] = chosen

    ranked = [(ref, j) for ref in (own, inner, far) for j in range(owned)]

    mine = mixes.at[c]

    def close(r, left, right):
        if right and r in closing:
            mix_copy(c, closing[r]).start()
        if left and r in lifting:
            late_copy(c, lifting[r]).start()

    def mid_actions():
        raw_nodes = [base + j for base in (near_mid, far_end * owned) for j in range(owned)]
        known = [home + j for j in range(owned)], [end * owned + j for j in range(owned)]
        raw_table = weights_for(home, known[0] + raw_nodes + known[1])
        tables = {}

        def prepare_tables():
            places = slots_of(raw_nodes, end)
            nodes = []
            for i in range(2 * owned):
                node = jnp.int32(0)
                for place, name in zip(places, raw_nodes):
                    node = jnp.where(place == i, name, node)
                nodes.append(node)
            tables["own"] = weights_for(home, known[0] + nodes + known[1])
            tables["end"] = weights_for(end * owned, known[0] + nodes + known[1])
            tables["places"] = slots_of(known[0] + known[1], far_end)

        def near(r):
            own_copy(r).wait_recv()
            if r < RAW:
                for i in range(owned):
                    pick(near_pick, i, i, r, ranked[: owned + 1 + i])
            else:
                rights_only = [row[: 2 * owned] + row[3 * owned :] for row in tables["end"][owned:]]
                blend(near_pick, r, rights_only, (own, inner, outer))
            near_copy(r).start()

        def far_in(r):
            pass_copy(r).wait_recv()
            if r < RAW:
                for i in range(owned):
                    pick(far_pick, i, owned + i, r, ranked[: 2 * owned + 1 + i])
            else:
                blend(far_pick, r, tables["end"][:owned], (own, inner, far, outer))
            far_copy(r).start()
            blend(mine, r, raw_table if r < RAW else tables["own"], (own, inner, far, outer))
            close(r, True, True)

        def pass_on(k):
            raw_copy(k).wait_recv()
            inside = [p for p, (at, _) in enumerate(pieces) if raws[k][0] <= at < sum(raws[k])]
            for p in inside:
                if p < RAW:
                    pass_copy(p).start()
                    continue
                if "places" not in tables:
                    prepare_tables()
                for m in range(2):
                    parts = [ref[m, j, rows(p)] for ref in (own, outer) for j in range(owned)]
                    for i in range(2 * owned):
                        chosen = parts[0]
                        for place, part in zip(tables["places"][1:], parts[1:]):
                            chosen = jnp.where(place == i, part, chosen)
                        (near_slot if i < owned else far_slot)[m, i % owned, rows(p)] = chosen
                near_slot_copy(p).start()
            if k == len(raws) - 1:
                for p in range(RAW, count):
                    far_slot_copy(p).start()

        return {"near": near, "far": far_in, "pass": pass_on}

    def end_actions():
        table = weights_for(home, [home + j for j in range(owned)] + spot_nodes)

        def near(r):
            near_copy(r).wait_recv()
            if r >= RAW:
                mixes[c, :, owned:, rows(r)] = inner[:, :, rows(r)]
                close(r, False, True)

        def far_in(r):
            far_copy(r).wait_recv()
            if r < RAW:
                blend(mine, r, table, (own, inner, far))
            else:
                mixes[c, :, :owned, rows(r)] = far[:, :, rows(r)]
            close(r, True, r < RAW)

        return {"near": near, "far": far_in}

    def clear():
        out_ref[...] = jnp.zeros_like(out_ref)

    def put_right(ref, h, k):
        span = pl.ds(*groups[k])
        for j in range(owned):
            re, im = ref[0, j, span], ref[1, j, span]
            for k, value in enumerate((re, im, re + im)):
                for i, part in enumerate(split(value)):
                    rights[j, 2 * k + i, h, span] = part

    def put_left(ref, h, n):
        re, im = ref[0, n], ref[1, n]
        for k, value in enumerate((re, im, re + im)):
            high, low_part = split(value)
            at, size = slices[0]
            lefts[n, 2 * k, h] = high[:, at : at + size]
            lefts[n, 2 * k + 1, h] = low_part[:, at : at + size]
            for i, (at, size) in enumerate(slices[1:]):
                part = high[:, at : at + size]
                packs[n, k, h, i] = jnp.concatenate([part, low_part[:, at : at + size], part], axis=1)

    def prepare_facing(k):
        x_copy(k).wait_recv()
        face_copy(c, pl.ds(*groups[k])).start()
        put_right(facing, 1 - x, k)

    def prepare_left(n):
        put_left(own, c, n)
        if n == 0:
            c_copy(1 - c).wait_recv()
        put_left(held.at[1 - c], 1 - c, n)

    def right_of(n):
        return lambda i: rights[n, i].reshape(2 * height, height)

    def wide(ref, q, m, span):
        return jnp.concatenate([ref[h, m, q, span] for h in range(2)], axis=1)

    def turn(k):
        mix_copy(1 - c, k).wait_recv()
        span = pl.ds(*batches[k])
        for n in range(owned):
            q = owned + n
            parts = stacked_mul(wide(mixes, q, 0, span), wide(mixes, q, 1, span), right_of(choices[n]))
            for m in range(2):
                turned[n, m, span] = parts[m]
        turned_copy(k).start()

    def square(i):
        n, quarter = i % owned, i // owned
        away, at = quarter // 2, quarter % 2 * (height // 2)
        ref, h = (faced, 1 - x) if away else (held, x)
        if i == 2 * owned:
            face_copy(1 - c, pl.ds(0, height)).wait_recv()
        span = pl.ds(at, height // 2)
        left = [jnp.concatenate([ref[h2, m, n, span] for h2 in range(2)], axis=1) for m in range(2)]
        parts = plain_mul(left[0], left[1], right_of(choices[n]))
        for m in range(2):
            for k, part in enumerate(split(parts[m])):
                squares[n, 2 * m + k, h, span] = part

    def raise_up(k):
        span = pl.ds(*lifts[k])
        late_copy(1 - c, k).wait_recv()
        if k == len(lifts) - 1:
            late_copy(1 - c, k + 1).wait_recv()
        for n in range(owned):
            right = lambda i: squares[n, i].reshape(2 * height, height)
            parts = stacked_mul(wide(mixes, n, 0, span), wide(mixes, n, 1, span), right)
            for m in range(2):
                out_ref[m, n, span] = out_ref[m, n, span] + parts[m]

    def add_slice(ref, h, k):
        at, size = slices[k]
        for n in range(owned):
            r0, r1 = ref[n, 0, at : at + size], ref[n, 1, at : at + size]
            if k == 0:
                parts = sliced_mul(lambda i: lefts[n, i, h], r0, r1)
            else:
                parts = packed_mul(lambda i: packs[n, i, h, k - 1], r0, r1)
            for m in range(2):
                out_ref[m, n] = out_ref[m, n] + parts[m]

    def add_theirs(k):
        at, size = slices[k]
        span = pl.ds(at, size)
        remote(
            turned.at[:, :, span], turned_far.at[:, :, span], x_send.at[1], t_recv.at[k], across
        ).wait_recv()
        add_slice(turned_far, 1 - x, k)

    clear()
    local.wait()

    shared = {
        "right": lambda k: put_right(own, x, k),
        "left": prepare_left,
        "facing": prepare_facing,
        "turn": turn,
        "square": square,
        "up": raise_up,
        "mine": lambda k: add_slice(turned, x, k),
        "theirs": add_theirs,
    }

    def run(role, own_actions):
        actions = {**shared, **own_actions()}
        for name, i in plan_of(role, count):
            with jax.named_scope(f"{name}{i}"):
                actions[name](i)

    @pl.when(is_mid)
    def _():
        run("mid", mid_actions)

    @pl.when(is_end)
    def _():
        run("end", end_actions)

    remote(x_ref, facing, x_send.at[0], x_recv.at[0], across).wait_send()
    remote(turned, turned_far, x_send.at[1], t_recv.at[0], across).wait_send()
    c_copy(c).wait_send()
    remote(mixes.at[c], mixes.at[c], c_send.at[1], m_recv.at[0], twin).wait_send()
    face_copy(c, pl.ds(0, height)).wait_send()

    @pl.when(is_end)
    def _():
        remote(x_ref, outer, z_send.at[0], o_recv.at[0], toward_mid).wait_send()

    @pl.when(is_mid)
    def _():
        remote(x_ref, inner, z_send.at[0], z_recv.at[0, 0], toward_mid).wait_send()
        remote(outer, far, z_send.at[1], z_recv.at[1, 0], toward_mid).wait_send()
        remote(near_pick, inner, z_send.at[2], z_recv.at[0, 0], toward_end).wait_send()
        remote(far_pick, far, z_send.at[3], z_recv.at[1, 0], toward_end).wait_send()


def line_body(meson_nodes, term_nodes, weight_codes, resident_pick):
    length = lax.axis_size("node")
    _, owned, height, width = meson_nodes.shape
    terms = term_nodes.shape[0]
    block = (height, width)
    vmem = pl.BlockSpec(memory_space=pltpu.VMEM)
    dma = pltpu.SemaphoreType.DMA
    count = len(UNITS)
    whole = pltpu.VMEM((2, owned) + block, jnp.float32)
    return pl.pallas_call(
        functools.partial(line_kernel, length, owned, terms),
        out_shape=pltpu.VMEM(meson_nodes.shape, jnp.float32),
        in_specs=[pl.BlockSpec(memory_space=pl.ANY)] * 4,
        out_specs=vmem,
        scratch_shapes=[
            pltpu.SMEM((2, terms), jnp.int32),
            pltpu.SMEM(weight_codes.shape, jnp.int32),
            pltpu.SMEM(resident_pick.shape, jnp.int32),
        ]
        + [pltpu.VMEM((2, 2, owned) + block, jnp.float32)] * 2
        + [whole] * 7
        + [
            pltpu.VMEM((2, 2, 2 * owned) + block, jnp.float32),
            pltpu.VMEM((owned, 2) + block, jnp.float32),
            pltpu.VMEM((owned, 2) + block, jnp.float32),
            pltpu.VMEM((owned, 6, 2, height, width // 2), jnp.bfloat16),
            pltpu.VMEM((owned, 3, 2, 2, height, 3 * width // GROUPS), jnp.bfloat16),
            pltpu.VMEM((owned, 6, 2) + block, jnp.bfloat16),
            pltpu.VMEM((owned, 4, 2) + block, jnp.bfloat16),
            dma((4,)),
            dma((4,)),
            dma((2, count)),
            dma((2 * GROUPS,)),
            dma((2,)),
            dma((GROUPS,)),
            dma((3,)),
            dma((3,)),
            dma((owned,)),
            dma((len(BATCHES) + GROUPS + 2,)),
            pltpu.SemaphoreType.REGULAR((3,)),
        ],
        compiler_params=pltpu.CompilerParams(
            collective_id=0, has_side_effects=True, vmem_limit_bytes=58 << 20
        ),
    )(meson_nodes, term_nodes.T, weight_codes, resident_pick)


def body(meson_nodes, term_nodes, weight_codes, resident_pick):
    length, owned = lax.axis_size("node"), meson_nodes.shape[1]
    height = meson_nodes.shape[2]
    square = height == meson_nodes.shape[3]
    halves = lax.axis_size("sub") == 2 and lax.axis_size("rep") == 2
    fits = height % (8 * sum(UNITS)) == 0 and term_nodes.shape[0] <= (length - 2) * owned
    if square and halves and fits and owned == 2 and length == 4:
        return line_body(meson_nodes, term_nodes, weight_codes, resident_pick)
    return wide_body(meson_nodes, term_nodes, weight_codes, resident_pick)


def solution(mesh):
    in_specs = (P(None, ("grp", "node"), "sub", "rep"), P("grp", None), P("grp"), P("grp"))
    out_specs = P(None, ("grp", "node"), "sub", "rep")
    return jax.shard_map(body, mesh=mesh, in_specs=in_specs, out_specs=out_specs, check_vma=False)
```
